32 devices in a mesh: seq: 8 (over z, x), head: 4 (over y, core).
Axes of the slice: x: 2, y: 2, z: 4, core: 2. Of those that a mesh axis runs over, the one named last changes fastest.
Arguments:
- hidden_states: bfloat16 [2, 352, 5120], P(None, 'seq', 'head'), may hold values from -60 to 60
- clean_states: bfloat16 [2, 352, 5120], P(None, 'seq', 'head'), may hold values from -60 to 60
- w_query: bfloat16 [5120, 2560], P(None, 'head'), may hold values from -2 to 2
- w_key: bfloat16 [5120, 2560], P(None, 'head'), may hold values from -2 to 2
- w_value: bfloat16 [5120, 2560], P(None, 'head'), may hold values from -0.078125 to 0.078125
- q_gain: float32 [2560], P('head'), may hold values from 0.1 to 1.9
- k_gain: float32 [2560], P('head'), may hold values from 0.1 to 1.9
- cache_keys: bfloat16 [9, 352, 2560], P(None, 'seq', 'head'), may hold values from -1300 to 1300
- cache_values: bfloat16 [9, 352, 2560], P(None, 'seq', 'head'), may hold values from -6 to 6
- modulation: float32 [4, 2, 5120], replicated, may hold values from -3 to 3
- controls: int32 [3], replicated, may hold values from 0 to 6, as said below
- frame_pos: int32 [11], replicated, may hold values from 0 to 63
Outputs:
- attention_out: bfloat16 [2, 352, 2560], P(None, 'seq', 'head')
- new_keys: bfloat16 [9, 352, 2560], P(None, 'seq', 'head')
- new_values: bfloat16 [9, 352, 2560], P(None, 'seq', 'head')
The draws below stay inside these ranges and needn't reach their ends.
Inputs may be any that keep to these rules, and one draw needn't show every extreme that they name: controls[0] lies in 1 to 3, controls[1] in 0 to 6 and equal to 6 whenever controls[0] is below 3, controls[2] in 1 to 2.
All inputs are finite; a program needn't handle non-finite values.
Results may differ from the reference program's by a relative error of at most 0.011.
The reference program's roundings to bfloat16 on the way count: a program that leaves them out, or rounds other values in their place, can miss the bound.
Values may be sent and summed in bfloat16 or wider, within the bound.
A program may use at most 320 MiB of HBM per device.

```python
import math
import jax
import jax.numpy as jnp
from jax import lax

D = 5120
HEADS = 20
HD = 128
CACHE_FRAMES = 9
GROUP_FRAMES = 2
STEPS = 4
INNER = 2560
FRAME = 352


def feature_draw(key, salt):
    key = jax.random.fold_in(key, salt)
    first_key, second_key = jax.random.split(key, 2)
    scales = jnp.exp(jax.random.uniform(first_key, (D,), jnp.float32) * math.log(10.0))
    base = jax.random.normal(second_key, (GROUP_FRAMES, FRAME, D), jnp.float32)
    return jnp.clip(base * scales[None, None, :], -60.0, 60.0).astype(jnp.bfloat16)


def column_draw(key, salt):
    key = jax.random.fold_in(key, salt)
    first_key, second_key = jax.random.split(key, 2)
    ramp = jnp.arange(INNER, dtype=jnp.float32) / max(INNER - 1, 1)
    scales = jnp.exp(jax.random.uniform(first_key, (INNER,), jnp.float32) * math.log(10.0)) * jnp.power(3.0, 0.5 * ramp)
    base = jax.random.normal(second_key, (D, INNER), jnp.float32)
    return jnp.clip(base * scales[None, :] / (3.0 * math.sqrt(D)), -2.0, 2.0).astype(jnp.bfloat16)


def draw_hidden_states(key, part):
    return feature_draw(key, 101)


def draw_clean_states(key, part):
    return feature_draw(key, 202)


def draw_w_query(key, part):
    return column_draw(key, 303)


def draw_w_key(key, part):
    return column_draw(key, 404)


def draw_cache_keys(key, part):
    key = jax.random.fold_in(key, 505)
    first_key = jax.random.fold_in(key, 0)
    base = jnp.clip(jax.random.normal(first_key, (CACHE_FRAMES, FRAME, INNER), jnp.float32), -6.0, 6.0)
    return base.astype(jnp.bfloat16)


def draw_controls(key, part):
    key = jax.random.fold_in(key, 606)
    step_key, slot_key, sink_key = jax.random.split(key, 3)
    step_value = jax.random.randint(step_key, (1,), 1, STEPS, jnp.int32)
    free_slot = jax.random.randint(slot_key, (1,), 0, 7, jnp.int32)
    slot_value = jnp.where(step_value < STEPS - 1, jnp.int32(6), free_slot).astype(jnp.int32)
    sink_value = jax.random.randint(sink_key, (1,), 1, 3, jnp.int32)
    return jnp.concatenate([step_value, slot_value, sink_value], axis=0)


def touch_ends(array, stream_key, smallest, largest):
    shape = array.shape
    spot = [jax.random.randint(jax.random.fold_in(stream_key, axis), (), 0, shape[axis]) for axis in range(len(shape))]
    array = array.at[tuple(spot)].set(smallest)
    longest = shape.index(max(shape))
    spot[longest] = (spot[longest] + 1) % shape[longest]
    return array.at[tuple(spot)].set(largest)


def level_of(own_key, shape, cuts, smallest, high):
    def one(dim, blocks):
        steps = jax.random.uniform(jax.random.fold_in(jax.random.fold_in(own_key, 6), dim), (blocks,), jnp.float32, smallest / len(cuts), high / len(cuts))
        return jnp.repeat(jnp.exp(steps), shape[dim] // blocks).reshape((-1,) + (1,) * (len(shape) - dim - 1))

    loudness = one(*cuts[0])
    for cut in cuts[1:]:
        loudness = loudness * one(*cut)
    return loudness


def normal_values(stream_key, shape, scale, reach, cuts=(), kind=jnp.bfloat16):
    result = scale * jax.random.normal(stream_key, shape, jnp.float32)
    if cuts:
        result = result * level_of(stream_key, shape, cuts, -0.22, 0.18)
    return jnp.clip(result, -reach, reach).astype(kind)


def setup_inputs(seed: int = 0) -> dict:
    keys = jax.random.split(jax.random.key(seed), 13)
    return {
        "hidden_states": draw_hidden_states(jax.random.fold_in(keys[12], 71), 0),
        "clean_states": draw_clean_states(jax.random.fold_in(keys[12], 71), 0),
        "w_query": draw_w_query(jax.random.fold_in(keys[12], 71), 0),
        "w_key": draw_w_key(jax.random.fold_in(keys[12], 71), 0),
        "w_value": normal_values(keys[4], (D, INNER), D ** -0.5, 0.078125, ((1, 4),)),
        "q_gain": jnp.clip(1.0 + 0.18 * jax.random.normal(keys[5], (INNER,), jnp.float32), 0.1, 1.9),
        "k_gain": jnp.clip(1.0 + 0.18 * jax.random.normal(keys[6], (INNER,), jnp.float32), 0.1, 1.9),
        "cache_keys": draw_cache_keys(jax.random.fold_in(keys[12], 71), 0),
        "cache_values": normal_values(keys[8], (CACHE_FRAMES, FRAME, INNER), 1.0, 6.0, ((1, 8), (2, 4))),
        "modulation": normal_values(keys[9], (STEPS, 2, D), 0.5, 3.0, (), jnp.float32),
        "controls": draw_controls(jax.random.fold_in(keys[12], 71), 0),
        "frame_pos": touch_ends(jax.random.randint(keys[11], (CACHE_FRAMES + GROUP_FRAMES,), 0, 64), jax.random.fold_in(keys[11], 1), 0, 63).astype(jnp.int32),
    }


epsilon = 1e-06

def modulate(states, modulation, step_index):
    choose = (jnp.arange(modulation.shape[0], dtype=jnp.int32) == step_index).astype(jnp.float32)
    picked = lax.optimization_barrier(jnp.sum(choose[:, None, None] * modulation, axis=0))
    values = states.astype(jnp.float32)
    centre = lax.optimization_barrier(jnp.mean(values, axis=-1, keepdims=True))
    spread = lax.optimization_barrier(jnp.mean(jnp.square(values - centre), axis=-1, keepdims=True))
    normed = (values - centre) * lax.rsqrt(spread + epsilon)
    return (normed * (1.0 + picked[1]) + picked[0]).astype(jnp.bfloat16)

def rms_scale(values, square_total, width, gain):
    return values * lax.rsqrt(square_total / width + epsilon)[:, None] * gain

def rotate(values, time_pos, space_pos):
    head_size = values.shape[-1]
    half_size = head_size // 2
    time_pairs = (head_size - 4 * (head_size // 6)) // 2
    space_pairs = half_size - time_pairs
    pair_index = jnp.arange(half_size, dtype=jnp.int32)
    exponent = jnp.where(pair_index < time_pairs, pair_index / time_pairs, (pair_index - time_pairs) / space_pairs).astype(jnp.float32)
    frequency = jnp.power(10000.0, -exponent)
    is_time = (pair_index < time_pairs)[None, None, :]
    position = jnp.where(is_time, time_pos.astype(jnp.float32)[:, None, None], space_pos.astype(jnp.float32)[None, :, None])
    angle = position * frequency
    cosine = jnp.cos(angle)[:, :, None, :]
    sine = jnp.sin(angle)[:, :, None, :]
    first = values[..., :half_size]
    second = values[..., half_size:]
    return jnp.concatenate([first * cosine - second * sine, second * cosine + first * sine], axis=-1)

def write_cache(key_store, value_store, fresh_keys, fresh_values, slot_start, sinks):
    rolling = key_store.shape[0] - sinks
    for group_frame in range(fresh_keys.shape[0]):
        target = (sinks + (slot_start + group_frame) % rolling).astype(jnp.int32)
        anchor = (target, jnp.int32(0), jnp.int32(0))
        key_store = lax.dynamic_update_slice(key_store, fresh_keys[group_frame:group_frame + 1], anchor)
        value_store = lax.dynamic_update_slice(value_store, fresh_values[group_frame:group_frame + 1], anchor)
    return (key_store, value_store)

def one_head(operands):
    query_head, key_head, value_head = operands
    scores = jnp.dot(query_head, key_head.T, preferred_element_type=jnp.float32) * HD ** (-0.5)
    top_score = lax.optimization_barrier(jnp.max(scores, axis=-1))
    weights = jnp.exp(scores - top_score[:, None])
    totals = lax.optimization_barrier(jnp.sum(weights, axis=-1))
    summed = jnp.dot(weights.astype(jnp.bfloat16), value_head, preferred_element_type=jnp.float32)
    return (summed / totals[:, None]).astype(jnp.bfloat16)

def reference(hidden_states, clean_states, w_query, w_key, w_value, q_gain, k_gain, cache_keys, cache_values, modulation, controls, frame_pos):
    timestep = controls[0]
    write_slot = controls[1]
    sink_count = controls[2]
    all_rows = GROUP_FRAMES * FRAME
    noisy = modulate(hidden_states, modulation, timestep).reshape(all_rows, D)
    settled = modulate(clean_states, modulation, jnp.int32(0)).reshape(all_rows, D)
    query_raw = jnp.dot(noisy, w_query, preferred_element_type=jnp.float32)
    key_raw = jnp.dot(noisy, w_key, preferred_element_type=jnp.float32)
    key_clean = jnp.dot(settled, w_key, preferred_element_type=jnp.float32)
    value_new = jnp.dot(noisy, w_value, preferred_element_type=jnp.float32).astype(jnp.bfloat16)
    value_clean = jnp.dot(settled, w_value, preferred_element_type=jnp.float32).astype(jnp.bfloat16)
    query_norm = rms_scale(query_raw, lax.optimization_barrier(jnp.sum(query_raw * query_raw, axis=-1)), INNER, q_gain)
    key_norm = rms_scale(key_raw, lax.optimization_barrier(jnp.sum(key_raw * key_raw, axis=-1)), INNER, k_gain)
    stored_keys = rms_scale(key_clean, lax.optimization_barrier(jnp.sum(key_clean * key_clean, axis=-1)), INNER, k_gain).astype(jnp.bfloat16)
    space_pos = jnp.arange(FRAME, dtype=jnp.int32)
    group_time = frame_pos[CACHE_FRAMES:]
    cache_time = frame_pos[:CACHE_FRAMES]
    query_rot = rotate(query_norm.reshape(GROUP_FRAMES, FRAME, HEADS, HD), group_time, space_pos).astype(jnp.bfloat16)
    key_rot = rotate(key_norm.reshape(GROUP_FRAMES, FRAME, HEADS, HD), group_time, space_pos).astype(jnp.bfloat16)
    cache_rot = rotate(cache_keys.astype(jnp.float32).reshape(CACHE_FRAMES, FRAME, HEADS, HD), cache_time, space_pos).astype(jnp.bfloat16)
    keys_all = jnp.concatenate([cache_rot.reshape(-1, HEADS, HD), key_rot.reshape(-1, HEADS, HD)], axis=0)
    values_all = jnp.concatenate([cache_values.reshape(-1, HEADS, HD), value_new.reshape(-1, HEADS, HD)], axis=0)
    attended = lax.map(one_head, (jnp.transpose(query_rot.reshape(-1, HEADS, HD), (1, 0, 2)), jnp.transpose(keys_all, (1, 0, 2)), jnp.transpose(values_all, (1, 0, 2))))
    attention_out = jnp.transpose(attended, (1, 0, 2)).reshape(GROUP_FRAMES, FRAME, INNER)
    new_keys, new_values = write_cache(cache_keys, cache_values, stored_keys.reshape(GROUP_FRAMES, FRAME, INNER), value_clean.reshape(GROUP_FRAMES, FRAME, INNER), write_slot, sink_count)
    return (attention_out, new_keys, new_values)
```

```python
import functools

import jax
import jax.numpy as jnp
import numpy as np
from jax import lax
from jax.experimental import pallas as pl
from jax.experimental.pallas import tpu as pltpu
from jax.sharding import PartitionSpec as P

HD = 128
epsilon = 1e-06
NX = 2
F32 = jnp.float32
BF16 = jnp.bfloat16


def kernel(
    n_seq,
    n_head,
    x_noisy,
    x_clean,
    w_query,
    w_key,
    w_value,
    q_gain,
    k_gain,
    cache_keys,
    cache_values,
    modulation,
    frequency,
    controls,
    frame_pos,
    out_ref,
    new_keys,
    new_values,
    w_vmem,
    xg,
    y,
    acc,
    acc_b,
    table,
    k32,
    v32,
    kb,
    vb,
    q_buf,
    part_send,
    part_recv,
    stat_send,
    stat_recv,
    ss_send,
    ss_recv,
    w_sem,
    x_send_sem,
    x_fwd_sem,
    x_recv_sem,
    ss_send_sem,
    ss_recv_sem,
    q_send_sem,
    q_fwd_sem,
    q_recv_sem,
    p_send_sem,
    p_recv_sem,
    t_send_sem,
    t_recv_sem,
):
    seq = lax.axis_index("seq")
    head = lax.axis_index("head")
    groups, frame, shard = x_noisy.shape
    padded = y.shape[2] // groups
    rows = groups * padded
    caches = cache_keys.shape[0]
    inner = w_query.shape[1]
    heads = inner // HD
    n_keys = (caches + groups) * frame
    key_rows = k32.shape[0]
    width = inner * n_head
    model = shard * n_head
    n_z = n_seq // NX
    n_y = n_head // 2
    z = seq // NX
    x = seq % NX
    mate_x = z * NX + (1 - x)
    core = head % 2
    yy = head // 2
    mate = yy * 2 + (1 - core)

    barrier = pltpu.get_barrier_semaphore()
    for step in range(1, n_head):
        pl.semaphore_signal(
            barrier, inc=1, device_id={"head": lax.rem(head + step, n_head)},
            device_id_type=pl.DeviceIdType.MESH,
        )
    for step in range(1, n_seq):
        pl.semaphore_signal(
            barrier, inc=1, device_id={"seq": lax.rem(seq + step, n_seq)},
            device_id_type=pl.DeviceIdType.MESH,
        )
    w_copies = [
        pltpu.make_async_copy(w, w_vmem.at[i], w_sem.at[i])
        for i, w in enumerate((w_query, w_key, w_value))
    ]
    for copy in w_copies:
        copy.start()
    pl.semaphore_wait(barrier, n_head - 1 + n_seq - 1)

    def remote(src, dst, send, recv, axis, index):
        return pltpu.make_async_remote_copy(
            src_ref=src, dst_ref=dst, send_sem=send, recv_sem=recv,
            device_id={axis: index}, device_id_type=pl.DeviceIdType.MESH,
        )

    def x_copy(kind, source, slot, send, to):
        return remote(source, xg.at[kind, slot], send, x_recv_sem.at[kind, slot], "head", to)

    own_x = (x_noisy, x_clean)
    x_sends = []
    for kind in range(2):
        for step in range(1, n_y):
            to = lax.rem(yy + step, n_y) * 2 + core
            x_sends.append(x_copy(kind, own_x[kind], head, x_send_sem.at[kind, step], to))
            x_sends[-1].start()
        x_sends.append(x_copy(kind, own_x[kind], head, x_send_sem.at[kind, 0], mate))
        x_sends[-1].start()
        xg[kind, head] = own_x[kind][...]

    y[...] = jnp.zeros_like(y)
    k32[n_keys:, :] = jnp.zeros((key_rows - n_keys, inner), F32)
    v32[n_keys:, :] = jnp.zeros((key_rows - n_keys, inner), F32)

    lane = lax.broadcasted_iota(jnp.int32, (padded, HD), 1)
    half = HD // 2
    time_pairs = (HD - 4 * (HD // 6)) // 2
    is_time = (lane % half) < time_pairs
    sign = jnp.where(lane < half, -1.0, 1.0).astype(F32)
    freq = frequency[0:1, :]
    space = (lax.broadcasted_iota(jnp.int32, (padded, HD), 0) + seq * frame).astype(F32)
    space_angle = space * freq
    space_cos = jnp.cos(space_angle)
    space_sin = jnp.sin(space_angle) * sign
    time_row = lax.broadcasted_iota(jnp.int32, (16, HD), 0)
    times = jnp.zeros((16, HD), F32)
    for f in range(caches + groups):
        times = jnp.where(time_row == f, frame_pos[f].astype(F32), times)
    time_angle = times * freq
    time_cos = jnp.cos(time_angle)
    time_sin = jnp.sin(time_angle) * sign[0:1, :]
    for f in range(caches + groups):
        table[f, 0] = jnp.where(is_time, time_cos[f : f + 1, :], space_cos)
        table[f, 1] = jnp.where(is_time, time_sin[f : f + 1, :], space_sin)

    def rotate(values, f, count):
        return values * table[f, 0, :count, :] + pltpu.roll(values, half, 1) * table[f, 1, :count, :]

    for f in range(caches):
        for h in range(heads):
            cols = slice(h * HD, (h + 1) * HD)
            at = slice(f * frame, (f + 1) * frame)
            k32[at, cols] = rotate(cache_keys[f, :, cols].astype(F32), f, frame)
            v32[at, cols] = cache_values[f, :, cols].astype(F32)

    def gather_x(kind):
        forwards = []
        for step in range(1, n_y):
            source = lax.rem(yy + n_y - step, n_y) * 2 + core
            x_copy(kind, own_x[kind], source, x_send_sem.at[kind, 0], mate).wait_recv()
            forwards.append(
                x_copy(kind, xg.at[kind, source], source, x_fwd_sem.at[kind, step], mate)
            )
            forwards[-1].start()
        for step in range(n_y):
            source = lax.rem(yy + n_y - step, n_y) * 2 + (1 - core)
            x_copy(kind, own_x[kind], source, x_send_sem.at[kind, 0], mate).wait_recv()
        return forwards

    def modulate(kind, step_index):
        def pick(part, columns):
            chosen = jnp.zeros((1, shard), F32)
            for i in range(modulation.shape[0]):
                chosen = jnp.where(step_index == i, modulation[i, part : part + 1, columns], chosen)
            return chosen

        for g in range(groups):
            total = jnp.zeros((frame, 1), F32)
            for j in range(n_head):
                total += jnp.sum(xg[kind, j, g].astype(F32), axis=-1, keepdims=True)
            centre = total / model
            total = jnp.zeros((frame, 1), F32)
            for j in range(n_head):
                away = xg[kind, j, g].astype(F32) - centre
                total += jnp.sum(away * away, axis=-1, keepdims=True)
            inverse = lax.rsqrt(total / model + epsilon)
            for j in range(n_head):
                columns = slice(j * shard, (j + 1) * shard)
                normed = (xg[kind, j, g].astype(F32) - centre) * inverse
                result = normed * (1.0 + pick(1, columns)) + pick(0, columns)
                y[kind, j, g * padded : g * padded + frame, :] = result.astype(BF16)

    def project(kind, which, target):
        target[...] = jnp.zeros_like(target)

        @pl.loop(0, n_head)
        def _(j):
            begin = pl.multiple_of(j * shard, shard)
            target[...] += jnp.dot(
                y[kind, j], w_vmem[which, pl.ds(begin, shard), :], preferred_element_type=F32
            )

    lanes = lax.broadcasted_iota(jnp.int32, (rows, HD), 1)

    def share_squares(kind, squares):
        ss_send[kind] = squares
        copies = []
        for step in range(1, n_head):
            to = lax.rem(head + step, n_head)
            copies.append(
                remote(
                    ss_send.at[kind], ss_recv.at[kind, head], ss_send_sem.at[kind, step],
                    ss_recv_sem.at[kind, head], "head", to,
                )
            )
            copies[-1].start()
        return copies

    def total_squares(kind, squares):
        for step in range(1, n_head):
            source = lax.rem(head + step, n_head)
            remote(
                ss_send.at[kind], ss_recv.at[kind, source], ss_send_sem.at[kind, step],
                ss_recv_sem.at[kind, source], "head", source,
            ).wait_recv()
            squares = squares + ss_recv[kind, source]
        return lax.rsqrt(squares / width + epsilon)

    forwards = gather_x(0)
    modulate(0, controls[0])
    w_copies[0].wait()
    project(0, 0, acc)
    w_copies[1].wait()
    project(0, 1, acc_b)
    query_squares = jnp.sum(acc[...] * acc[...], axis=-1, keepdims=True)
    key_squares = jnp.sum(acc_b[...] * acc_b[...], axis=-1, keepdims=True)
    squares = jnp.where(lanes == 0, query_squares, key_squares)
    ss_copies = share_squares(0, squares)
    inverse = total_squares(0, squares)
    for g in range(groups):
        at = slice(g * padded, (g + 1) * padded)
        query_scale = inverse[at, 0:1]
        for h in range(heads):
            cols = slice(h * HD, (h + 1) * HD)
            normed = acc[at, cols] * query_scale * q_gain[:, cols]
            q_buf[seq, at, cols] = rotate(normed, caches + g, padded).astype(BF16)

    def q_copy(source, send, to):
        return remote(q_buf.at[source], q_buf.at[source], send, q_recv_sem.at[source], "seq", to)

    q_sends = []
    for step in range(1, n_z):
        q_sends.append(q_copy(seq, q_send_sem.at[step], lax.rem(z + step, n_z) * NX + x))
        q_sends[-1].start()
    q_sends.append(q_copy(seq, q_fwd_sem.at[0], mate_x))
    q_sends[-1].start()

    for g in range(groups):
        at = slice(g * padded, (g + 1) * padded)
        key_scale = inverse[at, 1:2]
        place = slice((caches + g) * frame, (caches + g + 1) * frame)
        for h in range(heads):
            cols = slice(h * HD, (h + 1) * HD)
            normed = acc_b[at, cols] * key_scale * k_gain[:, cols]
            k32[place, cols] = rotate(normed, caches + g, padded)[:frame, :]
    w_copies[2].wait()
    project(0, 2, acc)
    for g in range(groups):
        place = slice((caches + g) * frame, (caches + g + 1) * frame)
        v32[place, :] = acc[g * padded : g * padded + frame, :]
    kb[...] = k32[...].astype(BF16)
    vb[...] = v32[...].astype(BF16)

    forwards += gather_x(1)
    modulate(1, jnp.int32(0))
    project(1, 1, acc_b)
    squares = jnp.broadcast_to(jnp.sum(acc_b[...] * acc_b[...], axis=-1, keepdims=True), (rows, HD))
    ss_copies += share_squares(1, squares)
    project(1, 2, acc)

    scale = HD ** (-0.5)
    column = lax.broadcasted_iota(jnp.int32, (rows, key_rows), 1)

    def attend(source, part, stat):
        stats = jnp.zeros((rows, HD), F32)
        for h in range(heads):
            cols = slice(h * HD, (h + 1) * HD)
            scores = lax.dot_general(
                q_buf[source, :, cols], kb[:, cols], (((1,), (1,)), ((), ())),
                preferred_element_type=F32,
            ) * scale
            scores = jnp.where(column < n_keys, scores, -3.0e38)
            top = jnp.max(scores, axis=-1, keepdims=True)
            weights = jnp.exp(scores - top)
            total = jnp.sum(weights, axis=-1, keepdims=True)
            part[:, cols] = jnp.dot(
                weights.astype(BF16), vb[:, cols], preferred_element_type=F32
            ).astype(BF16)
            stats = jnp.where(lanes == h, top, stats)
            stats = jnp.where(lanes == half + h, total, stats)
        stat[...] = stats

    def part_copy(slot, to):
        return (
            remote(
                part_send.at[to], part_recv.at[slot], p_send_sem.at[to], p_recv_sem.at[slot],
                "seq", to,
            ),
            remote(
                stat_send.at[to], stat_recv.at[slot], t_send_sem.at[to], t_recv_sem.at[slot],
                "seq", to,
            ),
        )

    @pl.loop(0, n_seq)
    def _(c):
        step = c // NX
        across = c % NX
        there = lax.rem(z + n_z - step, n_z) * NX
        source = there + lax.rem(x + across, NX)

        @pl.when(c > 0)
        def _():
            q_copy(source, q_send_sem.at[0], mate_x).wait_recv()

        @pl.when((c > 0) & (across == 0))
        def _():
            q_copy(source, q_fwd_sem.at[step], mate_x).start()

        attend(source, part_send.at[source], stat_send.at[source])

        @pl.when(c > 0)
        def _():
            for copy in part_copy(seq, source):
                copy.start()

    part_recv[seq] = part_send[seq]
    stat_recv[seq] = stat_send[seq]

    inverse = total_squares(1, squares)
    rolling = caches - controls[2]
    targets = [controls[2] + lax.rem(controls[1] + g, rolling) for g in range(groups)]
    for h in range(heads):
        cols = slice(h * HD, (h + 1) * HD)
        fresh = []
        for g in range(groups):
            at = slice(g * padded, (g + 1) * padded)
            normed = acc_b[at, cols] * inverse[at, 0:1] * k_gain[:, cols]
            fresh.append(
                (normed[:frame, :].astype(BF16), acc[at, cols][:frame, :].astype(BF16))
            )
        for f in range(caches):
            keys = cache_keys[f, :, cols]
            values = cache_values[f, :, cols]
            for g in range(groups):
                keys = jnp.where(targets[g] == f, fresh[g][0], keys)
                values = jnp.where(targets[g] == f, fresh[g][1], values)
            new_keys[f, :, cols] = keys
            new_values[f, :, cols] = values

    @pl.loop(1, n_seq)
    def _(c):
        source = lax.rem(seq + c, n_seq)
        for copy in part_copy(source, source):
            copy.wait_recv()

    def highest(j, top):
        return jnp.maximum(top, stat_recv[j])

    top = lax.fori_loop(1, n_seq, highest, stat_recv[0])

    def summed(j, total):
        stat = stat_recv[j]
        weight = jnp.exp(stat - top)
        for h in range(heads):
            cols = slice(h * HD, (h + 1) * HD)
            acc[:, cols] += part_recv[j, :, cols].astype(F32) * weight[:, h : h + 1]
        return total + weight * pltpu.roll(stat, half, 1)

    acc[...] = jnp.zeros_like(acc)
    total = lax.fori_loop(0, n_seq, summed, jnp.zeros((rows, HD), F32))
    for h in range(heads):
        cols = slice(h * HD, (h + 1) * HD)
        result = (acc[:, cols] / total[:, h : h + 1]).astype(BF16)
        for g in range(groups):
            out_ref[g, :, cols] = result[g * padded : g * padded + frame, :]

    for copy in x_sends + forwards + ss_copies + q_sends:
        copy.wait_send()

    @pl.loop(1, n_z)
    def _(step):
        source = lax.rem(z + n_z - step, n_z) * NX + x
        q_copy(source, q_fwd_sem.at[step], mate_x).wait_send()

    @pl.loop(1, n_seq)
    def _(c):
        source = lax.rem(seq + c, n_seq)
        for copy in part_copy(seq, source):
            copy.wait_send()


def body(n_seq, n_head, hidden, clean, w_query, w_key, w_value, q_gain, k_gain, keys, values,
         modulation, controls, frame_pos):
    groups, frame, shard = hidden.shape
    caches = keys.shape[0]
    inner = w_query.shape[1]
    padded = -(-frame // 16) * 16
    rows = groups * padded
    key_rows = -(-((caches + groups) * frame) // 128) * 128
    half = HD // 2
    time_pairs = (HD - 4 * (HD // 6)) // 2
    pair = np.arange(half)
    exponent = np.where(pair < time_pairs, pair / time_pairs, (pair - time_pairs) / (half - time_pairs))
    line = np.power(10000.0, -exponent).astype(np.float32)
    frequency = jnp.asarray(np.tile(np.concatenate([line, line])[None, :], (8, 1)))
    vmem = pl.BlockSpec(memory_space=pltpu.VMEM)
    smem = pl.BlockSpec(memory_space=pltpu.SMEM)
    hbm = pl.BlockSpec(memory_space=pl.ANY)
    dma = pltpu.SemaphoreType.DMA
    return pl.pallas_call(
        functools.partial(kernel, n_seq, n_head),
        out_shape=(
            jax.ShapeDtypeStruct((groups, frame, inner), BF16),
            jax.ShapeDtypeStruct(keys.shape, BF16),
            jax.ShapeDtypeStruct(values.shape, BF16),
        ),
        in_specs=[vmem, vmem, hbm, hbm, hbm, vmem, vmem, vmem, vmem, vmem, vmem, smem, smem],
        out_specs=(vmem, vmem, vmem),
        scratch_shapes=[
            pltpu.VMEM((3,) + w_query.shape, BF16),
            pltpu.VMEM((2, n_head, groups, frame, shard), BF16),
            pltpu.VMEM((2, n_head, rows, shard), BF16),
            pltpu.VMEM((rows, inner), F32),
            pltpu.VMEM((rows, inner), F32),
            pltpu.VMEM((caches + groups, 2, padded, HD), F32),
            pltpu.VMEM((key_rows, inner), F32),
            pltpu.VMEM((key_rows, inner), F32),
            pltpu.VMEM((key_rows, inner), BF16),
            pltpu.VMEM((key_rows, inner), BF16),
            pltpu.VMEM((n_seq, rows, inner), BF16),
            pltpu.VMEM((n_seq, rows, inner), BF16),
            pltpu.VMEM((n_seq, rows, inner), BF16),
            pltpu.VMEM((n_seq, rows, HD), F32),
            pltpu.VMEM((n_seq, rows, HD), F32),
            pltpu.VMEM((2, rows, HD), F32),
            pltpu.VMEM((2, n_head, rows, HD), F32),
            dma((3,)),
            dma((2, n_head)),
            dma((2, n_head)),
            dma((2, n_head)),
            dma((2, n_head)),
            dma((2, n_head)),
            dma((n_seq,)),
            dma((n_seq,)),
            dma((n_seq,)),
            dma((n_seq,)),
            dma((n_seq,)),
            dma((n_seq,)),
            dma((n_seq,)),
        ],
        compiler_params=pltpu.CompilerParams(
            collective_id=0, has_side_effects=True, vmem_limit_bytes=60 * 1024 * 1024
        ),
        name="block",
    )(hidden, clean, w_query, w_key, w_value, q_gain[None, :], k_gain[None, :], keys, values,
      modulation, frequency, controls, frame_pos)


def solution(mesh):
    split = P(None, "seq", "head")
    columns = P(None, "head")
    in_specs = (
        split, split, columns, columns, columns, P("head"), P("head"), split, split, P(), P(), P(),
    )
    step = functools.partial(body, mesh.shape["seq"], mesh.shape["head"])
    return jax.shard_map(
        step, mesh=mesh, in_specs=in_specs, out_specs=(split, split, split), check_vma=False
    )
```

```python
import functools

import jax
import jax.numpy as jnp
import numpy as np
from jax import lax
from jax.experimental import pallas as pl
from jax.experimental.pallas import tpu as pltpu
from jax.sharding import PartitionSpec as P

HD = 128
epsilon = 1e-06
NX = 2
F32 = jnp.float32
BF16 = jnp.bfloat16


def kernel(
    n_seq,
    n_head,
    x_noisy,
    x_clean,
    w_query,
    w_key,
    w_value,
    q_gain,
    k_gain,
    cache_keys,
    cache_values,
    modulation,
    frequency,
    controls,
    frame_pos,
    out_ref,
    fresh_keys,
    fresh_values,
    w_vmem,
    mod_vmem,
    keys_vmem,
    values_vmem,
    xg,
    y,
    acc,
    acc_b,
    table,
    k32,
    v32,
    kb,
    vb,
    q_buf,
    part_send,
    part_recv,
    stat_send,
    stat_recv,
    ss_send,
    ss_recv,
    own_part,
    own_stat,
    part_mate,
    stat_mate,
    mate_in,
    mate_stat,
    w_sem,
    in_sem,
    x_send_sem,
    x_fwd_sem,
    x_recv_sem,
    ss_send_sem,
    ss_recv_sem,
    q_send_sem,
    q_fwd_sem,
    q_recv_sem,
    p_send_sem,
    p_recv_sem,
    t_send_sem,
    t_recv_sem,
    m_send_sem,
    m_recv_sem,
    mt_send_sem,
    mt_recv_sem,
):
    seq = lax.axis_index("seq")
    head = lax.axis_index("head")
    groups, frame, shard = x_noisy.shape
    padded = y.shape[2] // groups
    rows = groups * padded
    caches = cache_keys.shape[0]
    inner = w_query.shape[1]
    heads = inner // HD
    n_keys = (caches + groups) * frame
    key_rows = k32.shape[0]
    width = inner * n_head
    model = shard * n_head
    link_rows = ss_send.shape[-1]
    n_z = n_seq // NX
    n_y = n_head // 2
    z = seq // NX
    x = seq % NX
    mate_x = z * NX + (1 - x)
    core = head % 2
    yy = head // 2
    mate = yy * 2 + (1 - core)

    barrier = pltpu.get_barrier_semaphore()
    for step in range(1, n_head):
        pl.semaphore_signal(
            barrier, inc=1, device_id={"head": lax.rem(head + step, n_head)},
            device_id_type=pl.DeviceIdType.MESH,
        )
    for step in range(1, n_seq):
        pl.semaphore_signal(
            barrier, inc=1, device_id={"seq": lax.rem(seq + step, n_seq)},
            device_id_type=pl.DeviceIdType.MESH,
        )
    w_copies = [
        pltpu.make_async_copy(w, w_vmem.at[i], w_sem.at[i])
        for i, w in enumerate((w_query, w_key, w_value))
    ]
    in_copies = [
        pltpu.make_async_copy(source, target, in_sem.at[i])
        for i, (source, target) in enumerate((
            (x_noisy, xg.at[0, head]), (x_clean, xg.at[1, head]), (modulation, mod_vmem),
            (cache_keys, keys_vmem), (cache_values, values_vmem),
        ))
    ]
    for copy in in_copies:
        copy.start()
    for copy in w_copies:
        copy.start()
    pl.semaphore_wait(barrier, n_head - 1 + n_seq - 1)

    def remote(src, dst, send, recv, axis, index):
        return pltpu.make_async_remote_copy(
            src_ref=src, dst_ref=dst, send_sem=send, recv_sem=recv,
            device_id={axis: index}, device_id_type=pl.DeviceIdType.MESH,
        )

    def x_copy(kind, source, slot, send, to):
        return remote(source, xg.at[kind, slot], send, x_recv_sem.at[kind, slot], "head", to)

    own_x = (x_noisy, x_clean)
    x_sends = []
    for kind in range(2):
        for step in range(1, n_y):
            to = lax.rem(yy + step, n_y) * 2 + core
            x_sends.append(x_copy(kind, own_x[kind], head, x_send_sem.at[kind, step], to))
            x_sends[-1].start()
        x_sends.append(x_copy(kind, own_x[kind], head, x_send_sem.at[kind, 0], mate))
        x_sends[-1].start()

    y[...] = jnp.zeros_like(y)
    k32[n_keys:, :] = jnp.zeros((key_rows - n_keys, inner), F32)
    v32[n_keys:, :] = jnp.zeros((key_rows - n_keys, inner), F32)

    lane = lax.broadcasted_iota(jnp.int32, (padded, HD), 1)
    half = HD // 2
    time_pairs = (HD - 4 * (HD // 6)) // 2
    is_time = (lane % half) < time_pairs
    sign = jnp.where(lane < half, -1.0, 1.0).astype(F32)
    freq = frequency[0:1, :]
    space = (lax.broadcasted_iota(jnp.int32, (padded, HD), 0) + seq * frame).astype(F32)
    space_angle = space * freq
    space_cos = jnp.cos(space_angle)
    space_sin = jnp.sin(space_angle) * sign
    time_row = lax.broadcasted_iota(jnp.int32, (16, HD), 0)
    times = jnp.zeros((16, HD), F32)
    for f in range(caches + groups):
        times = jnp.where(time_row == f, frame_pos[f].astype(F32), times)
    time_angle = times * freq
    time_cos = jnp.cos(time_angle)
    time_sin = jnp.sin(time_angle) * sign[0:1, :]
    for f in range(caches + groups):
        table[f, 0] = jnp.where(is_time, time_cos[f : f + 1, :], space_cos)
        table[f, 1] = jnp.where(is_time, time_sin[f : f + 1, :], space_sin)

    def rotate(values, f, count):
        return values * table[f, 0, :count, :] + pltpu.roll(values, half, 1) * table[f, 1, :count, :]

    in_copies[3].wait()
    in_copies[4].wait()
    for f in range(caches):
        for h in range(heads):
            cols = slice(h * HD, (h + 1) * HD)
            at = slice(f * frame, (f + 1) * frame)
            k32[at, cols] = rotate(keys_vmem[f, :, cols].astype(F32), f, frame)
            v32[at, cols] = values_vmem[f, :, cols].astype(F32)

    def gather_x(kind):
        forwards = []
        for step in range(1, n_y):
            source = lax.rem(yy + n_y - step, n_y) * 2 + core
            x_copy(kind, own_x[kind], source, x_send_sem.at[kind, 0], mate).wait_recv()
            forwards.append(
                x_copy(kind, xg.at[kind, source], source, x_fwd_sem.at[kind, step], mate)
            )
            forwards[-1].start()
        for step in range(n_y):
            source = lax.rem(yy + n_y - step, n_y) * 2 + (1 - core)
            x_copy(kind, own_x[kind], source, x_send_sem.at[kind, 0], mate).wait_recv()
        return forwards

    def modulate(kind, step_index):
        def pick(part, columns):
            chosen = jnp.zeros((1, shard), F32)
            for i in range(mod_vmem.shape[0]):
                chosen = jnp.where(step_index == i, mod_vmem[i, part : part + 1, columns], chosen)
            return chosen

        for g in range(groups):
            total = jnp.zeros((frame, 1), F32)
            for j in range(n_head):
                total += jnp.sum(xg[kind, j, g].astype(F32), axis=-1, keepdims=True)
            centre = total / model
            total = jnp.zeros((frame, 1), F32)
            for j in range(n_head):
                away = xg[kind, j, g].astype(F32) - centre
                total += jnp.sum(away * away, axis=-1, keepdims=True)
            inverse = lax.rsqrt(total / model + epsilon)
            for j in range(n_head):
                columns = slice(j * shard, (j + 1) * shard)
                normed = (xg[kind, j, g].astype(F32) - centre) * inverse
                result = normed * (1.0 + pick(1, columns)) + pick(0, columns)
                y[kind, j, g * padded : g * padded + frame, :] = result.astype(BF16)

    def project(kind, which, target):
        target[...] = jnp.zeros_like(target)

        @pl.loop(0, n_head)
        def _(j):
            begin = pl.multiple_of(j * shard, shard)
            target[...] += jnp.dot(
                y[kind, j], w_vmem[which, pl.ds(begin, shard), :], preferred_element_type=F32
            )

    lanes = lax.broadcasted_iota(jnp.int32, (rows, HD), 1)

    def to_link(stats):
        tall = jnp.concatenate([stats, jnp.zeros((link_rows - rows, HD), F32)], axis=0)
        return tall.T[:16, :]

    def from_link(flat):
        tall = jnp.concatenate([flat, jnp.zeros((HD - 16, link_rows), F32)], axis=0)
        return tall.T[:rows, :]

    def share_squares(kind, values):
        squares = jnp.sum(values * values, axis=-1, keepdims=True)
        flat = to_link(jnp.broadcast_to(squares, (rows, HD)))
        ss_send[kind] = flat
        copies = []
        for step in range(1, n_head):
            to = lax.rem(head + step, n_head)
            copies.append(
                remote(
                    ss_send.at[kind], ss_recv.at[kind, head], ss_send_sem.at[kind, step],
                    ss_recv_sem.at[kind, head], "head", to,
                )
            )
            copies[-1].start()
        return copies, flat

    def total_squares(kind, squares):
        for step in range(1, n_head):
            source = lax.rem(head + step, n_head)
            remote(
                ss_send.at[kind], ss_recv.at[kind, source], ss_send_sem.at[kind, step],
                ss_recv_sem.at[kind, source], "head", source,
            ).wait_recv()
            squares = squares + ss_recv[kind, source]
        return from_link(lax.rsqrt(squares / width + epsilon))[:, 0:1]

    in_copies[0].wait()
    in_copies[2].wait()
    forwards = gather_x(0)
    modulate(0, controls[0])
    w_copies[0].wait()
    project(0, 0, acc)
    ss_copies, squares = share_squares(0, acc[...])
    w_copies[1].wait()
    project(0, 1, acc_b)
    more, key_squares = share_squares(1, acc_b[...])
    ss_copies += more
    inverse = total_squares(0, squares)
    for g in range(groups):
        at = slice(g * padded, (g + 1) * padded)
        for h in range(heads):
            cols = slice(h * HD, (h + 1) * HD)
            normed = acc[at, cols] * inverse[at, :] * q_gain[:, cols]
            q_buf[seq, at, cols] = rotate(normed, caches + g, padded).astype(BF16)

    def q_copy(source, send, to):
        return remote(q_buf.at[source], q_buf.at[source], send, q_recv_sem.at[source], "seq", to)

    q_sends = []
    for step in range(1, n_z):
        q_sends.append(q_copy(seq, q_send_sem.at[step], lax.rem(z + step, n_z) * NX + x))
        q_sends[-1].start()
    q_sends.append(q_copy(seq, q_fwd_sem.at[0], mate_x))
    q_sends[-1].start()

    w_copies[2].wait()
    project(0, 2, acc)
    inverse = total_squares(1, key_squares)
    for g in range(groups):
        at = slice(g * padded, (g + 1) * padded)
        place = slice((caches + g) * frame, (caches + g + 1) * frame)
        v32[place, :] = acc[at, :][:frame, :]
        for h in range(heads):
            cols = slice(h * HD, (h + 1) * HD)
            normed = acc_b[at, cols] * inverse[at, :] * k_gain[:, cols]
            k32[place, cols] = rotate(normed, caches + g, padded)[:frame, :]
    kb[...] = k32[...].astype(BF16)
    vb[...] = v32[...].astype(BF16)

    in_copies[1].wait()
    forwards += gather_x(1)
    modulate(1, jnp.int32(0))
    project(1, 1, acc_b)
    more, clean_squares = share_squares(2, acc_b[...])
    ss_copies += more

    sharp = HD ** (-0.5) * 1.4426950408889634
    last = key_rows - HD
    column = lax.broadcasted_iota(jnp.int32, (NX * rows, HD), 1) + last
    wide = lax.broadcasted_iota(jnp.int32, (NX * rows, HD), 1)

    def attend(there, slot):
        stats = jnp.zeros((NX * rows, HD), F32)
        queries = q_buf[pl.ds(there, NX)].reshape(NX * rows, inner)
        for h in range(heads):
            cols = slice(h * HD, (h + 1) * HD)
            scores = lax.dot_general(
                queries[:, cols], kb[:, cols], (((1,), (1,)), ((), ())),
                preferred_element_type=F32,
            )
            edge = jnp.where(column < n_keys, scores[:, last:], -3.0e38)
            scores = jnp.concatenate([scores[:, :last], edge], axis=1)
            top = jnp.max(scores, axis=-1, keepdims=True)
            weights = jnp.exp2((scores - top) * sharp)
            total = jnp.sum(weights, axis=-1, keepdims=True)
            sums = jnp.dot(weights.astype(BF16), vb[:, cols], preferred_element_type=F32)
            own_part[slot, :, :, cols] = sums.reshape(NX, rows, HD)
            stats = jnp.where(wide == h, top, stats)
            stats = jnp.where(wide == 8 + h, total, stats)
        own_stat[slot] = stats.reshape(NX, rows, HD)

    def mate_copy(step):
        return (
            remote(
                part_mate.at[step], mate_in.at[step], m_send_sem.at[step], m_recv_sem.at[step],
                "seq", mate_x,
            ),
            remote(
                stat_mate.at[step], mate_stat.at[step], mt_send_sem.at[step],
                mt_recv_sem.at[step], "seq", mate_x,
            ),
        )

    def part_copy(from_z, to_z):
        to = to_z * NX + x
        return (
            remote(
                part_send.at[to_z], part_recv.at[from_z], p_send_sem.at[to_z],
                p_recv_sem.at[from_z], "seq", to,
            ),
            remote(
                stat_send.at[to_z], stat_recv.at[from_z], t_send_sem.at[to_z],
                t_recv_sem.at[from_z], "seq", to,
            ),
        )

    @pl.loop(0, n_z + 1)
    def _(step):
        @pl.when(step < n_z)
        def _():
            there = lax.rem(z + n_z - step, n_z) * NX

            @pl.when(step > 0)
            def _():
                q_copy(there + x, q_send_sem.at[0], mate_x).wait_recv()
                q_copy(there + x, q_fwd_sem.at[step], mate_x).start()

            q_copy(there + (1 - x), q_send_sem.at[0], mate_x).wait_recv()
            slot = lax.rem(step, 2)
            attend(there, slot)
            part_mate[step] = own_part[slot, 1 - x].astype(BF16)
            stat_mate[step] = to_link(own_stat[slot, 1 - x])
            for copy in mate_copy(step):
                copy.start()

        @pl.when(step > 0)
        def _():
            done = step - 1
            slot = lax.rem(done, 2)
            to_z = lax.rem(z + n_z - done, n_z)
            for copy in mate_copy(done):
                copy.wait_recv()
            mine = own_stat[slot, x]
            other = from_link(mate_stat[done])
            top = jnp.maximum(mine, other)
            weight = jnp.exp2((mine - top) * sharp)
            weight_other = jnp.exp2((other - top) * sharp)
            total = weight * pltpu.roll(mine, HD - 8, 1) + weight_other * pltpu.roll(other, HD - 8, 1)
            stats = jnp.where(lanes < 8, top, pltpu.roll(total, 8, 1))
            for h in range(heads):
                cols = slice(h * HD, (h + 1) * HD)
                part_send[to_z, :, cols] = (
                    own_part[slot, x, :, cols] * weight[:, h : h + 1]
                    + mate_in[done, :, cols].astype(F32) * weight_other[:, h : h + 1]
                ).astype(BF16)
            stat_send[to_z] = to_link(stats)

            @pl.when(done > 0)
            def _():
                for copy in part_copy(z, to_z):
                    copy.start()

    part_recv[z] = part_send[z]
    stat_recv[z] = stat_send[z]

    project(1, 2, acc)
    inverse = total_squares(2, clean_squares)
    for g in range(groups):
        at = slice(g * padded, (g + 1) * padded)
        normed = acc_b[at, :] * inverse[at, :] * k_gain[...]
        fresh_keys[g] = normed[:frame, :].astype(BF16)
        fresh_values[g] = acc[at, :][:frame, :].astype(BF16)

    @pl.loop(1, n_z)
    def _(c):
        source = lax.rem(z + c, n_z)
        for copy in part_copy(source, source):
            copy.wait_recv()

    stats = [from_link(stat_recv[j]) for j in range(n_z)]
    top = stats[0]
    for stat in stats[1:]:
        top = jnp.maximum(top, stat)
    total = jnp.zeros((rows, HD), F32)
    acc[...] = jnp.zeros_like(acc)
    for j in range(n_z):
        weight = jnp.exp2((stats[j] - top) * sharp)
        total = total + weight * pltpu.roll(stats[j], HD - 8, 1)
        for h in range(heads):
            cols = slice(h * HD, (h + 1) * HD)
            acc[:, cols] += part_recv[j, :, cols].astype(F32) * weight[:, h : h + 1]
    for h in range(heads):
        cols = slice(h * HD, (h + 1) * HD)
        result = (acc[:, cols] / total[:, h : h + 1]).astype(BF16)
        for g in range(groups):
            out_ref[g, :, cols] = result[g * padded : g * padded + frame, :]

    for copy in x_sends + forwards + ss_copies + q_sends:
        copy.wait_send()

    @pl.loop(1, n_z)
    def _(step):
        source = lax.rem(z + n_z - step, n_z) * NX + x
        q_copy(source, q_fwd_sem.at[step], mate_x).wait_send()

    @pl.loop(1, n_z)
    def _(c):
        to_z = lax.rem(z + c, n_z)
        for copy in part_copy(z, to_z):
            copy.wait_send()

    @pl.loop(0, n_z)
    def _(step):
        for copy in mate_copy(step):
            copy.wait_send()


def write_kernel(controls, keys, values, fresh_keys, fresh_values, new_keys, new_values):
    caches, groups = keys.shape[0], fresh_keys.shape[0]
    rolling = caches - controls[2]
    targets = [controls[2] + lax.rem(controls[1] + g, rolling) for g in range(groups)]
    for old, fresh, new in ((keys, fresh_keys, new_keys), (values, fresh_values, new_values)):
        for f in range(caches):
            kept = old[f]
            for g in range(groups):
                kept = jnp.where(targets[g] == f, fresh[g], kept)
            new[f] = kept


def body(n_seq, n_head, hidden, clean, w_query, w_key, w_value, q_gain, k_gain, keys, values,
         modulation, controls, frame_pos):
    groups, frame, shard = hidden.shape
    caches = keys.shape[0]
    inner = w_query.shape[1]
    padded = -(-frame // 16) * 16
    rows = groups * padded
    key_rows = -(-((caches + groups) * frame) // 128) * 128
    half = HD // 2
    time_pairs = (HD - 4 * (HD // 6)) // 2
    pair = np.arange(half)
    exponent = np.where(pair < time_pairs, pair / time_pairs, (pair - time_pairs) / (half - time_pairs))
    line = np.power(10000.0, -exponent).astype(np.float32)
    frequency = jnp.asarray(np.tile(np.concatenate([line, line])[None, :], (8, 1)))
    vmem = pl.BlockSpec(memory_space=pltpu.VMEM)
    smem = pl.BlockSpec(memory_space=pltpu.SMEM)
    hbm = pl.BlockSpec(memory_space=pl.ANY)
    dma = pltpu.SemaphoreType.DMA
    n_z = n_seq // NX
    link_rows = -(-rows // 128) * 128
    fresh = jax.ShapeDtypeStruct((groups, frame, inner), BF16)
    out, fresh_keys, fresh_values = pl.pallas_call(
        functools.partial(kernel, n_seq, n_head),
        out_shape=(fresh, fresh, fresh),
        in_specs=[hbm, hbm, hbm, hbm, hbm, vmem, vmem, hbm, hbm, hbm, vmem, smem, smem],
        out_specs=(vmem, vmem, vmem),
        scratch_shapes=[
            pltpu.VMEM((3,) + w_query.shape, BF16),
            pltpu.VMEM(modulation.shape, F32),
            pltpu.VMEM(keys.shape, BF16),
            pltpu.VMEM(values.shape, BF16),
            pltpu.VMEM((2, n_head, groups, frame, shard), BF16),
            pltpu.VMEM((2, n_head, rows, shard), BF16),
            pltpu.VMEM((rows, inner), F32),
            pltpu.VMEM((rows, inner), F32),
            pltpu.VMEM((caches + groups, 2, padded, HD), F32),
            pltpu.VMEM((key_rows, inner), F32),
            pltpu.VMEM((key_rows, inner), F32),
            pltpu.VMEM((key_rows, inner), BF16),
            pltpu.VMEM((key_rows, inner), BF16),
            pltpu.VMEM((n_seq, rows, inner), BF16),
            pltpu.VMEM((n_z, rows, inner), BF16),
            pltpu.VMEM((n_z, rows, inner), BF16),
            pltpu.VMEM((n_z, 16, link_rows), F32),
            pltpu.VMEM((n_z, 16, link_rows), F32),
            pltpu.VMEM((3, 16, link_rows), F32),
            pltpu.VMEM((3, n_head, 16, link_rows), F32),
            pltpu.VMEM((2, NX, rows, inner), F32),
            pltpu.VMEM((2, NX, rows, HD), F32),
            pltpu.VMEM((n_z, rows, inner), BF16),
            pltpu.VMEM((n_z, 16, link_rows), F32),
            pltpu.VMEM((n_z, rows, inner), BF16),
            pltpu.VMEM((n_z, 16, link_rows), F32),
            dma((3,)),
            dma((5,)),
            dma((2, n_head)),
            dma((2, n_head)),
            dma((2, n_head)),
            dma((3, n_head)),
            dma((3, n_head)),
            dma((n_seq,)),
            dma((n_seq,)),
            dma((n_seq,)),
            dma((n_z,)),
            dma((n_z,)),
            dma((n_z,)),
            dma((n_z,)),
            dma((n_z,)),
            dma((n_z,)),
            dma((n_z,)),
            dma((n_z,)),
        ],
        compiler_params=pltpu.CompilerParams(
            collective_id=0, has_side_effects=True, vmem_limit_bytes=60 * 1024 * 1024
        ),
        name="block",
    )(hidden, clean, w_query, w_key, w_value, q_gain[None, :], k_gain[None, :], keys, values,
      modulation, frequency, controls, frame_pos)
    new_keys, new_values = pl.pallas_call(
        write_kernel,
        out_shape=(
            jax.ShapeDtypeStruct(keys.shape, BF16),
            jax.ShapeDtypeStruct(values.shape, BF16),
        ),
        in_specs=[smem, vmem, vmem, vmem, vmem],
        out_specs=(vmem, vmem),
        name="write",
    )(controls, keys, values, fresh_keys, fresh_values)
    return out, new_keys, new_values


def solution(mesh):
    split = P(None, "seq", "head")
    columns = P(None, "head")
    in_specs = (
        split, split, columns, columns, columns, P("head"), P("head"), split, split, P(), P(), P(),
    )
    step = functools.partial(body, mesh.shape["seq"], mesh.shape["head"])
    return jax.shard_map(
        step, mesh=mesh, in_specs=in_specs, out_specs=(split, split, split), check_vma=False
    )
```

```python
import functools

import jax
import jax.numpy as jnp
import numpy as np
from jax import lax
from jax.experimental import pallas as pl
from jax.experimental.pallas import tpu as pltpu
from jax.sharding import PartitionSpec as P

HD = 128
epsilon = 1e-06
NX = 2
F32 = jnp.float32
BF16 = jnp.bfloat16


def kernel(
    n_seq,
    n_head,
    x_noisy,
    x_clean,
    w_query,
    w_key,
    w_value,
    q_gain,
    k_gain,
    cache_keys,
    cache_values,
    modulation,
    frequency,
    controls,
    frame_pos,
    out_ref,
    fresh_keys,
    fresh_values,
    w_vmem,
    mod_vmem,
    keys_vmem,
    values_vmem,
    xg,
    y,
    acc,
    acc_b,
    table,
    k32,
    v32,
    kb,
    vb,
    q_buf,
    part_send,
    part_recv,
    stat_send,
    stat_recv,
    ss_send,
    ss_recv,
    own_part,
    own_stat,
    part_mate,
    stat_mate,
    mate_in,
    mate_stat,
    w_sem,
    in_sem,
    x_send_sem,
    x_fwd_sem,
    x_recv_sem,
    ss_send_sem,
    ss_recv_sem,
    q_send_sem,
    q_fwd_sem,
    q_recv_sem,
    p_send_sem,
    p_recv_sem,
    t_send_sem,
    t_recv_sem,
    m_send_sem,
    m_recv_sem,
    mt_send_sem,
    mt_recv_sem,
):
    seq = lax.axis_index("seq")
    head = lax.axis_index("head")
    groups, frame, shard = x_noisy.shape
    padded = y.shape[2] // groups
    rows = groups * padded
    caches = cache_keys.shape[0]
    inner = w_query.shape[1]
    heads = inner // HD
    n_keys = (caches + groups) * frame
    key_rows = k32.shape[0]
    width = inner * n_head
    model = shard * n_head
    link_rows = ss_send.shape[-1]
    n_z = n_seq // NX
    n_y = n_head // 2
    z = seq // NX
    x = seq % NX
    mate_x = z * NX + (1 - x)
    core = head % 2
    yy = head // 2
    mate = yy * 2 + (1 - core)

    def partner(step):
        if n_z & (n_z - 1):
            return lax.rem(z + step, n_z)
        other, bit = 0, 1
        while bit < n_z:
            other = other + (z // bit + step // bit) % 2 * bit
            bit *= 2
        return other

    def source_z(step):
        return lax.rem(z + n_z - step, n_z) if n_z & (n_z - 1) else partner(step)

    barrier = pltpu.get_barrier_semaphore()
    for step in range(1, n_head):
        pl.semaphore_signal(
            barrier, inc=1, device_id={"head": lax.rem(head + step, n_head)},
            device_id_type=pl.DeviceIdType.MESH,
        )
    for step in range(1, n_seq):
        pl.semaphore_signal(
            barrier, inc=1, device_id={"seq": lax.rem(seq + step, n_seq)},
            device_id_type=pl.DeviceIdType.MESH,
        )
    w_copies = [
        pltpu.make_async_copy(w, w_vmem.at[i], w_sem.at[i])
        for i, w in enumerate((w_query, w_key, w_value))
    ]
    in_copies = [
        pltpu.make_async_copy(source, target, in_sem.at[i])
        for i, (source, target) in enumerate((
            (x_noisy, xg.at[0, head]), (x_clean, xg.at[1, head]), (modulation, mod_vmem),
            (cache_keys, keys_vmem), (cache_values, values_vmem),
        ))
    ]
    for copy in in_copies:
        copy.start()
    for copy in w_copies:
        copy.start()
    pl.semaphore_wait(barrier, n_head - 1 + n_seq - 1)

    def remote(src, dst, send, recv, axis, index):
        return pltpu.make_async_remote_copy(
            src_ref=src, dst_ref=dst, send_sem=send, recv_sem=recv,
            device_id={axis: index}, device_id_type=pl.DeviceIdType.MESH,
        )

    def x_copy(kind, source, slot, send, to):
        return remote(source, xg.at[kind, slot], send, x_recv_sem.at[kind, slot], "head", to)

    own_x = (x_noisy, x_clean)
    x_sends = []
    for kind in range(2):
        for step in range(1, n_y):
            to = lax.rem(yy + step, n_y) * 2 + core
            x_sends.append(x_copy(kind, own_x[kind], head, x_send_sem.at[kind, step], to))
            x_sends[-1].start()
        x_sends.append(x_copy(kind, own_x[kind], head, x_send_sem.at[kind, 0], mate))
        if kind == 0:
            x_sends[-1].start()

    y[...] = jnp.zeros_like(y)
    k32[n_keys:, :] = jnp.zeros((key_rows - n_keys, inner), F32)
    v32[n_keys:, :] = jnp.zeros((key_rows - n_keys, inner), F32)

    lane = lax.broadcasted_iota(jnp.int32, (padded, HD), 1)
    half = HD // 2
    time_pairs = (HD - 4 * (HD // 6)) // 2
    is_time = (lane % half) < time_pairs
    sign = jnp.where(lane < half, -1.0, 1.0).astype(F32)
    freq = frequency[0:1, :]
    space = (lax.broadcasted_iota(jnp.int32, (padded, HD), 0) + seq * frame).astype(F32)
    space_angle = space * freq
    space_cos = jnp.cos(space_angle)
    space_sin = jnp.sin(space_angle) * sign
    time_row = lax.broadcasted_iota(jnp.int32, (16, HD), 0)
    times = jnp.zeros((16, HD), F32)
    for f in range(caches + groups):
        times = jnp.where(time_row == f, frame_pos[f].astype(F32), times)
    time_angle = times * freq
    time_cos = jnp.cos(time_angle)
    time_sin = jnp.sin(time_angle) * sign[0:1, :]
    for f in range(caches + groups):
        table[f, 0] = jnp.where(is_time, time_cos[f : f + 1, :], space_cos)
        table[f, 1] = jnp.where(is_time, time_sin[f : f + 1, :], space_sin)

    def rotate(values, f, count):
        return values * table[f, 0, :count, :] + pltpu.roll(values, half, 1) * table[f, 1, :count, :]

    in_copies[3].wait()
    in_copies[4].wait()
    for f in range(caches):
        for h in range(heads):
            cols = slice(h * HD, (h + 1) * HD)
            at = slice(f * frame, (f + 1) * frame)
            k32[at, cols] = rotate(keys_vmem[f, :, cols].astype(F32), f, frame)
            v32[at, cols] = values_vmem[f, :, cols].astype(F32)

    def gather_x(kind):
        forwards = []
        for step in range(1, n_y):
            source = lax.rem(yy + n_y - step, n_y) * 2 + core
            x_copy(kind, own_x[kind], source, x_send_sem.at[kind, 0], mate).wait_recv()
            forwards.append(
                x_copy(kind, xg.at[kind, source], source, x_fwd_sem.at[kind, step], mate)
            )
            forwards[-1].start()
        if kind == 0:
            x_sends[-1].start()
        for step in range(n_y):
            source = lax.rem(yy + n_y - step, n_y) * 2 + (1 - core)
            x_copy(kind, own_x[kind], source, x_send_sem.at[kind, 0], mate).wait_recv()
        return forwards

    def modulate(kind, step_index):
        def pick(part, columns):
            chosen = jnp.zeros((1, shard), F32)
            for i in range(mod_vmem.shape[0]):
                chosen = jnp.where(step_index == i, mod_vmem[i, part : part + 1, columns], chosen)
            return chosen

        for g in range(groups):
            total = jnp.zeros((frame, 1), F32)
            for j in range(n_head):
                total += jnp.sum(xg[kind, j, g].astype(F32), axis=-1, keepdims=True)
            centre = total / model
            total = jnp.zeros((frame, 1), F32)
            for j in range(n_head):
                away = xg[kind, j, g].astype(F32) - centre
                total += jnp.sum(away * away, axis=-1, keepdims=True)
            inverse = lax.rsqrt(total / model + epsilon)
            for j in range(n_head):
                columns = slice(j * shard, (j + 1) * shard)
                normed = (xg[kind, j, g].astype(F32) - centre) * inverse
                result = normed * (1.0 + pick(1, columns)) + pick(0, columns)
                y[kind, j, g * padded : g * padded + frame, :] = result.astype(BF16)

    def project(kind, which, target):
        target[...] = jnp.zeros_like(target)

        @pl.loop(0, n_head)
        def _(j):
            begin = pl.multiple_of(j * shard, shard)
            target[...] += jnp.dot(
                y[kind, j], w_vmem[which, pl.ds(begin, shard), :], preferred_element_type=F32
            )

    lanes = lax.broadcasted_iota(jnp.int32, (rows, HD), 1)

    def to_link(stats):
        tall = jnp.concatenate([stats, jnp.zeros((link_rows - rows, HD), F32)], axis=0)
        return tall.T[:16, :]

    def from_link(flat):
        tall = jnp.concatenate([flat, jnp.zeros((HD - 16, link_rows), F32)], axis=0)
        return tall.T[:rows, :]

    def share_squares(kind, values):
        squares = jnp.sum(values * values, axis=-1, keepdims=True)
        flat = to_link(jnp.broadcast_to(squares, (rows, HD)))
        ss_send[kind] = flat
        copies = []
        for step in range(1, n_head):
            to = lax.rem(head + step, n_head)
            copies.append(
                remote(
                    ss_send.at[kind], ss_recv.at[kind, head], ss_send_sem.at[kind, step],
                    ss_recv_sem.at[kind, head], "head", to,
                )
            )
            copies[-1].start()
        return copies, flat

    def total_squares(kind, squares):
        for step in range(1, n_head):
            source = lax.rem(head + step, n_head)
            remote(
                ss_send.at[kind], ss_recv.at[kind, source], ss_send_sem.at[kind, step],
                ss_recv_sem.at[kind, source], "head", source,
            ).wait_recv()
            squares = squares + ss_recv[kind, source]
        return from_link(lax.rsqrt(squares / width + epsilon))[:, 0:1]

    in_copies[0].wait()
    in_copies[2].wait()
    forwards = gather_x(0)
    modulate(0, controls[0])
    w_copies[0].wait()
    project(0, 0, acc)
    ss_copies, squares = share_squares(0, acc[...])
    w_copies[1].wait()
    project(0, 1, acc_b)
    more, key_squares = share_squares(1, acc_b[...])
    ss_copies += more
    inverse = total_squares(0, squares)
    for g in range(groups):
        at = slice(g * padded, (g + 1) * padded)
        for h in range(heads):
            cols = slice(h * HD, (h + 1) * HD)
            normed = acc[at, cols] * inverse[at, :] * q_gain[cols][None, :]
            q_buf[seq, at, cols] = rotate(normed, caches + g, padded).astype(BF16)

    def q_copy(source, send, to):
        return remote(q_buf.at[source], q_buf.at[source], send, q_recv_sem.at[source], "seq", to)

    q_sends = []
    for step in range(1, n_z):
        q_sends.append(q_copy(seq, q_send_sem.at[step], partner(step) * NX + x))
        q_sends[-1].start()
    q_sends.append(q_copy(seq, q_fwd_sem.at[0], mate_x))
    q_sends[-1].start()

    w_copies[2].wait()
    project(0, 2, acc)
    inverse = total_squares(1, key_squares)
    for g in range(groups):
        at = slice(g * padded, (g + 1) * padded)
        place = slice((caches + g) * frame, (caches + g + 1) * frame)
        v32[place, :] = acc[at, :][:frame, :]
        for h in range(heads):
            cols = slice(h * HD, (h + 1) * HD)
            normed = acc_b[at, cols] * inverse[at, :] * k_gain[cols][None, :]
            k32[place, cols] = rotate(normed, caches + g, padded)[:frame, :]
    kb[...] = k32[...].astype(BF16)
    vb[...] = v32[...].astype(BF16)

    def pass_on(step):
        source = source_z(step) * NX + x
        q_copy(source, q_send_sem.at[0], mate_x).wait_recv()
        q_copy(source, q_fwd_sem.at[step], mate_x).start()

    in_copies[1].wait()
    forwards += gather_x(1)
    modulate(1, jnp.int32(0))
    if n_z > 1:
        pass_on(1)
    project(1, 1, acc_b)
    more, clean_squares = share_squares(2, acc_b[...])
    ss_copies += more

    sharp = HD ** (-0.5) * 1.4426950408889634
    last = key_rows - HD
    column = lax.broadcasted_iota(jnp.int32, (NX * rows, HD), 1) + last
    wide = lax.broadcasted_iota(jnp.int32, (NX * rows, HD), 1)

    def attend(there, slot):
        stats = jnp.zeros((NX * rows, HD), F32)
        queries = q_buf[pl.ds(there, NX)].reshape(NX * rows, inner)
        for h in range(heads):
            cols = slice(h * HD, (h + 1) * HD)
            scores = lax.dot_general(
                queries[:, cols], kb[:, cols], (((1,), (1,)), ((), ())),
                preferred_element_type=F32,
            )
            edge = jnp.where(column < n_keys, scores[:, last:], -3.0e38)
            scores = jnp.concatenate([scores[:, :last], edge], axis=1)
            top = jnp.max(scores, axis=-1, keepdims=True)
            weights = jnp.exp2((scores - top) * sharp)
            total = jnp.sum(weights, axis=-1, keepdims=True)
            sums = jnp.dot(weights.astype(BF16), vb[:, cols], preferred_element_type=F32)
            own_part[slot, :, :, cols] = sums.reshape(NX, rows, HD)
            stats = jnp.where(wide == h, top, stats)
            stats = jnp.where(wide == 8 + h, total, stats)
        own_stat[slot] = stats.reshape(NX, rows, HD)

    def mate_copy(step):
        return (
            remote(
                part_mate.at[step], mate_in.at[step], m_send_sem.at[step], m_recv_sem.at[step],
                "seq", mate_x,
            ),
            remote(
                stat_mate.at[step], mate_stat.at[step], mt_send_sem.at[step],
                mt_recv_sem.at[step], "seq", mate_x,
            ),
        )

    def part_copy(from_z, to_z):
        to = to_z * NX + x
        return (
            remote(
                part_send.at[to_z], part_recv.at[from_z], p_send_sem.at[to_z],
                p_recv_sem.at[from_z], "seq", to,
            ),
            remote(
                stat_send.at[to_z], stat_recv.at[from_z], t_send_sem.at[to_z],
                t_recv_sem.at[from_z], "seq", to,
            ),
        )

    def merge(done):
        slot = lax.rem(done, 2)
        to_z = source_z(done)
        for copy in mate_copy(done):
            copy.wait_recv()
        mine = own_stat[slot, x]
        other = from_link(mate_stat[done])
        top = jnp.maximum(mine, other)
        weight = jnp.exp2((mine - top) * sharp)
        weight_other = jnp.exp2((other - top) * sharp)
        total = weight * pltpu.roll(mine, HD - 8, 1) + weight_other * pltpu.roll(other, HD - 8, 1)
        for h in range(heads):
            cols = slice(h * HD, (h + 1) * HD)
            part_send[to_z, :, cols] = (
                own_part[slot, x, :, cols] * weight[:, h : h + 1]
                + mate_in[done, :, cols].astype(F32) * weight_other[:, h : h + 1]
            ).astype(BF16)
        stat_send[to_z] = to_link(jnp.where(lanes < 8, top, pltpu.roll(total, 8, 1)))

    @pl.loop(0, n_z)
    def _(step):
        there = source_z(step) * NX
        q_copy(there + (1 - x), q_send_sem.at[0], mate_x).wait_recv()
        slot = lax.rem(step, 2)
        attend(there, slot)
        part_mate[step] = own_part[slot, 1 - x].astype(BF16)
        stat_mate[step] = to_link(own_stat[slot, 1 - x])
        for copy in mate_copy(step):
            copy.start()

        @pl.when(step + 2 < n_z)
        def _():
            pass_on(step + 2)

        @pl.when(step > 0)
        def _():
            merge(step - 1)

            @pl.when(step > 1)
            def _():
                for copy in part_copy(z, source_z(step - 1)):
                    copy.start()

    project(1, 2, acc)
    inverse = total_squares(2, clean_squares)
    for g in range(groups):
        at = slice(g * padded, (g + 1) * padded)
        normed = acc_b[at, :] * inverse[at, :] * k_gain[...][None, :]
        fresh_keys[g] = normed[:frame, :].astype(BF16)
        fresh_values[g] = acc[at, :][:frame, :].astype(BF16)

    merge(n_z - 1)
    if n_z > 1:
        for copy in part_copy(z, source_z(n_z - 1)):
            copy.start()
    part_recv[z] = part_send[z]
    stat_recv[z] = stat_send[z]

    @pl.loop(1, n_z)
    def _(c):
        source = lax.rem(z + c, n_z)
        for copy in part_copy(source, source):
            copy.wait_recv()

    stats = [from_link(stat_recv[j]) for j in range(n_z)]
    top = stats[0]
    for stat in stats[1:]:
        top = jnp.maximum(top, stat)
    total = jnp.zeros((rows, HD), F32)
    acc[...] = jnp.zeros_like(acc)
    for j in range(n_z):
        weight = jnp.exp2((stats[j] - top) * sharp)
        total = total + weight * pltpu.roll(stats[j], HD - 8, 1)
        for h in range(heads):
            cols = slice(h * HD, (h + 1) * HD)
            acc[:, cols] += part_recv[j, :, cols].astype(F32) * weight[:, h : h + 1]
    for h in range(heads):
        cols = slice(h * HD, (h + 1) * HD)
        result = (acc[:, cols] / total[:, h : h + 1]).astype(BF16)
        for g in range(groups):
            out_ref[g, :, cols] = result[g * padded : g * padded + frame, :]

    for copy in x_sends + forwards + ss_copies + q_sends:
        copy.wait_send()

    @pl.loop(1, n_z)
    def _(step):
        q_copy(source_z(step) * NX + x, q_fwd_sem.at[step], mate_x).wait_send()

    @pl.loop(1, n_z)
    def _(c):
        to_z = lax.rem(z + c, n_z)
        for copy in part_copy(z, to_z):
            copy.wait_send()

    @pl.loop(0, n_z)
    def _(step):
        for copy in mate_copy(step):
            copy.wait_send()


def write_kernel(controls, keys, values, fresh_keys, fresh_values, new_keys, new_values):
    caches, groups = keys.shape[0], fresh_keys.shape[0]
    rolling = caches - controls[2]
    targets = [controls[2] + lax.rem(controls[1] + g, rolling) for g in range(groups)]
    for old, fresh, new in ((keys, fresh_keys, new_keys), (values, fresh_values, new_values)):
        for f in range(caches):
            kept = old[f]
            for g in range(groups):
                kept = jnp.where(targets[g] == f, fresh[g], kept)
            new[f] = kept


def body(n_seq, n_head, hidden, clean, w_query, w_key, w_value, q_gain, k_gain, keys, values,
         modulation, controls, frame_pos):
    groups, frame, shard = hidden.shape
    caches = keys.shape[0]
    inner = w_query.shape[1]
    padded = -(-frame // 16) * 16
    rows = groups * padded
    key_rows = -(-((caches + groups) * frame) // 128) * 128
    half = HD // 2
    time_pairs = (HD - 4 * (HD // 6)) // 2
    pair = np.arange(half)
    exponent = np.where(pair < time_pairs, pair / time_pairs, (pair - time_pairs) / (half - time_pairs))
    line = np.power(10000.0, -exponent).astype(np.float32)
    frequency = jnp.asarray(np.tile(np.concatenate([line, line])[None, :], (8, 1)))
    vmem = pl.BlockSpec(memory_space=pltpu.VMEM)
    smem = pl.BlockSpec(memory_space=pltpu.SMEM)
    hbm = pl.BlockSpec(memory_space=pl.ANY)
    dma = pltpu.SemaphoreType.DMA
    n_z = n_seq // NX
    link_rows = -(-rows // 128) * 128
    fresh = jax.ShapeDtypeStruct((groups, frame, inner), BF16)
    out, fresh_keys, fresh_values = pl.pallas_call(
        functools.partial(kernel, n_seq, n_head),
        out_shape=(fresh, fresh, fresh),
        in_specs=[hbm, hbm, hbm, hbm, hbm, vmem, vmem, hbm, hbm, hbm, vmem, smem, smem],
        out_specs=(vmem, vmem, vmem),
        scratch_shapes=[
            pltpu.VMEM((3,) + w_query.shape, BF16),
            pltpu.VMEM(modulation.shape, F32),
            pltpu.VMEM(keys.shape, BF16),
            pltpu.VMEM(values.shape, BF16),
            pltpu.VMEM((2, n_head, groups, frame, shard), BF16),
            pltpu.VMEM((2, n_head, rows, shard), BF16),
            pltpu.VMEM((rows, inner), F32),
            pltpu.VMEM((rows, inner), F32),
            pltpu.VMEM((caches + groups, 2, padded, HD), F32),
            pltpu.VMEM((key_rows, inner), F32),
            pltpu.VMEM((key_rows, inner), F32),
            pltpu.VMEM((key_rows, inner), BF16),
            pltpu.VMEM((key_rows, inner), BF16),
            pltpu.VMEM((n_seq, rows, inner), BF16),
            pltpu.VMEM((n_z, rows, inner), BF16),
            pltpu.VMEM((n_z, rows, inner), BF16),
            pltpu.VMEM((n_z, 16, link_rows), F32),
            pltpu.VMEM((n_z, 16, link_rows), F32),
            pltpu.VMEM((3, 16, link_rows), F32),
            pltpu.VMEM((3, n_head, 16, link_rows), F32),
            pltpu.VMEM((2, NX, rows, inner), F32),
            pltpu.VMEM((2, NX, rows, HD), F32),
            pltpu.VMEM((n_z, rows, inner), BF16),
            pltpu.VMEM((n_z, 16, link_rows), F32),
            pltpu.VMEM((n_z, rows, inner), BF16),
            pltpu.VMEM((n_z, 16, link_rows), F32),
            dma((3,)),
            dma((5,)),
            dma((2, n_head)),
            dma((2, n_head)),
            dma((2, n_head)),
            dma((3, n_head)),
            dma((3, n_head)),
            dma((n_seq,)),
            dma((n_seq,)),
            dma((n_seq,)),
            dma((n_z,)),
            dma((n_z,)),
            dma((n_z,)),
            dma((n_z,)),
            dma((n_z,)),
            dma((n_z,)),
            dma((n_z,)),
            dma((n_z,)),
        ],
        compiler_params=pltpu.CompilerParams(
            collective_id=0, has_side_effects=True, vmem_limit_bytes=60 * 1024 * 1024
        ),
        name="block",
    )(hidden, clean, w_query, w_key, w_value, q_gain, k_gain, keys, values,
      modulation, frequency, controls, frame_pos)
    new_keys, new_values = pl.pallas_call(
        write_kernel,
        out_shape=(
            jax.ShapeDtypeStruct(keys.shape, BF16),
            jax.ShapeDtypeStruct(values.shape, BF16),
        ),
        in_specs=[smem, vmem, vmem, vmem, vmem],
        out_specs=(vmem, vmem),
        name="write",
    )(controls, keys, values, fresh_keys, fresh_values)
    return out, new_keys, new_values


def solution(mesh):
    split = P(None, "seq", "head")
    columns = P(None, "head")
    in_specs = (
        split, split, columns, columns, columns, P("head"), P("head"), split, split, P(), P(), P(),
    )
    step = functools.partial(body, mesh.shape["seq"], mesh.shape["head"])
    return jax.shard_map(
        step, mesh=mesh, in_specs=in_specs, out_specs=(split, split, split), check_vma=False
    )
```

```python
import functools

import jax
import jax.numpy as jnp
import numpy as np
from jax import lax
from jax.experimental import pallas as pl
from jax.experimental.pallas import tpu as pltpu
from jax.sharding import PartitionSpec as P

HD = 128
epsilon = 1e-06
NX = 2
F32 = jnp.float32
BF16 = jnp.bfloat16


def kernel(
    n_seq,
    n_head,
    x_noisy,
    x_clean,
    w_query,
    w_key,
    w_value,
    q_gain,
    k_gain,
    cache_keys,
    cache_values,
    modulation,
    frequency,
    controls,
    frame_pos,
    out_ref,
    fresh_keys,
    fresh_values,
    w_vmem,
    mod_vmem,
    keys_vmem,
    values_vmem,
    xg,
    y,
    acc,
    acc_b,
    table,
    k32,
    v32,
    kb,
    vb,
    q_buf,
    part_send,
    part_recv,
    stat_send,
    stat_recv,
    ss_send,
    ss_recv,
    own_part,
    own_stat,
    part_mate,
    stat_mate,
    mate_in,
    mate_stat,
    w_sem,
    in_sem,
    x_send_sem,
    x_fwd_sem,
    x_recv_sem,
    ss_send_sem,
    ss_recv_sem,
    q_send_sem,
    q_fwd_sem,
    q_recv_sem,
    p_send_sem,
    p_recv_sem,
    t_send_sem,
    t_recv_sem,
    m_send_sem,
    m_recv_sem,
    mt_send_sem,
    mt_recv_sem,
):
    seq = lax.axis_index("seq")
    head = lax.axis_index("head")
    groups, frame, shard = x_noisy.shape
    padded = y.shape[2] // groups
    rows = groups * padded
    caches = cache_keys.shape[0]
    inner = w_query.shape[1]
    heads = inner // HD
    n_keys = (caches + groups) * frame
    key_rows = k32.shape[0]
    width = inner * n_head
    model = shard * n_head
    link_rows = ss_send.shape[-1]
    n_z = n_seq // NX
    n_y = n_head // 2
    z = seq // NX
    x = seq % NX
    mate_x = z * NX + (1 - x)
    core = head % 2
    yy = head // 2
    mate = yy * 2 + (1 - core)

    def partner(step):
        if n_z & (n_z - 1):
            return lax.rem(z + step, n_z)
        other, bit = 0, 1
        while bit < n_z:
            other = other + (z // bit + step // bit) % 2 * bit
            bit *= 2
        return other

    def source_z(step):
        return lax.rem(z + n_z - step, n_z) if n_z & (n_z - 1) else partner(step)

    barrier = pltpu.get_barrier_semaphore()
    for step in range(1, n_head):
        pl.semaphore_signal(
            barrier, inc=1, device_id={"head": lax.rem(head + step, n_head)},
            device_id_type=pl.DeviceIdType.MESH,
        )
    for step in range(1, n_seq):
        pl.semaphore_signal(
            barrier, inc=1, device_id={"seq": lax.rem(seq + step, n_seq)},
            device_id_type=pl.DeviceIdType.MESH,
        )
    w_copies = [
        pltpu.make_async_copy(w, w_vmem.at[i], w_sem.at[i])
        for i, w in enumerate((w_query, w_key, w_value))
    ]
    in_copies = [
        pltpu.make_async_copy(source, target, in_sem.at[i])
        for i, (source, target) in enumerate((
            (x_noisy, xg.at[0, head]), (x_clean, xg.at[1, head]), (modulation, mod_vmem),
            (cache_keys, keys_vmem), (cache_values, values_vmem),
        ))
    ]
    for copy in in_copies:
        copy.start()
    for copy in w_copies:
        copy.start()
    pl.semaphore_wait(barrier, n_head - 1 + n_seq - 1)

    def remote(src, dst, send, recv, axis, index):
        return pltpu.make_async_remote_copy(
            src_ref=src, dst_ref=dst, send_sem=send, recv_sem=recv,
            device_id={axis: index}, device_id_type=pl.DeviceIdType.MESH,
        )

    def x_copy(kind, source, slot, send, to):
        return remote(source, xg.at[kind, slot], send, x_recv_sem.at[kind, slot], "head", to)

    own_x = (x_noisy, x_clean)
    x_sends = []
    for kind in range(2):
        for step in range(1, n_y):
            to = lax.rem(yy + step, n_y) * 2 + core
            x_sends.append(x_copy(kind, own_x[kind], head, x_send_sem.at[kind, step], to))
            x_sends[-1].start()
        x_sends.append(x_copy(kind, own_x[kind], head, x_send_sem.at[kind, 0], mate))
        if kind == 0:
            x_sends[-1].start()

    y[...] = jnp.zeros_like(y)
    k32[n_keys:, :] = jnp.zeros((key_rows - n_keys, inner), F32)
    v32[n_keys:, :] = jnp.zeros((key_rows - n_keys, inner), F32)

    lane = lax.broadcasted_iota(jnp.int32, (padded, HD), 1)
    half = HD // 2
    time_pairs = (HD - 4 * (HD // 6)) // 2
    is_time = (lane % half) < time_pairs
    sign = jnp.where(lane < half, -1.0, 1.0).astype(F32)
    freq = frequency[0:1, :]
    space = (lax.broadcasted_iota(jnp.int32, (padded, HD), 0) + seq * frame).astype(F32)
    space_angle = space * freq
    space_cos = jnp.cos(space_angle)
    space_sin = jnp.sin(space_angle) * sign
    time_row = lax.broadcasted_iota(jnp.int32, (16, HD), 0)
    times = jnp.zeros((16, HD), F32)
    for f in range(caches + groups):
        times = jnp.where(time_row == f, frame_pos[f].astype(F32), times)
    time_angle = times * freq
    time_cos = jnp.cos(time_angle)
    time_sin = jnp.sin(time_angle) * sign[0:1, :]
    for f in range(caches + groups):
        table[f, 0] = jnp.where(is_time, time_cos[f : f + 1, :], space_cos)
        table[f, 1] = jnp.where(is_time, time_sin[f : f + 1, :], space_sin)

    def rotate(values, f, count):
        return values * table[f, 0, :count, :] + pltpu.roll(values, half, 1) * table[f, 1, :count, :]

    in_copies[3].wait()
    in_copies[4].wait()
    for f in range(caches):
        for h in range(heads):
            cols = slice(h * HD, (h + 1) * HD)
            at = slice(f * frame, (f + 1) * frame)
            k32[at, cols] = rotate(keys_vmem[f, :, cols].astype(F32), f, frame)
            v32[at, cols] = values_vmem[f, :, cols].astype(F32)

    def gather_x(kind):
        forwards = []
        for step in range(1, n_y):
            source = lax.rem(yy + n_y - step, n_y) * 2 + core
            x_copy(kind, own_x[kind], source, x_send_sem.at[kind, 0], mate).wait_recv()
            forwards.append(
                x_copy(kind, xg.at[kind, source], source, x_fwd_sem.at[kind, step], mate)
            )
            forwards[-1].start()
        if kind == 0:
            x_sends[-1].start()
        for step in range(n_y):
            source = lax.rem(yy + n_y - step, n_y) * 2 + (1 - core)
            x_copy(kind, own_x[kind], source, x_send_sem.at[kind, 0], mate).wait_recv()
        return forwards

    def modulate(kind, step_index):
        def pick(part, columns):
            chosen = jnp.zeros((1, shard), F32)
            for i in range(mod_vmem.shape[0]):
                chosen = jnp.where(step_index == i, mod_vmem[i, part : part + 1, columns], chosen)
            return chosen

        for g in range(groups):
            total = jnp.zeros((frame, 1), F32)
            for j in range(n_head):
                total += jnp.sum(xg[kind, j, g].astype(F32), axis=-1, keepdims=True)
            centre = total / model
            total = jnp.zeros((frame, 1), F32)
            for j in range(n_head):
                away = xg[kind, j, g].astype(F32) - centre
                total += jnp.sum(away * away, axis=-1, keepdims=True)
            inverse = lax.rsqrt(total / model + epsilon)
            for j in range(n_head):
                columns = slice(j * shard, (j + 1) * shard)
                normed = (xg[kind, j, g].astype(F32) - centre) * inverse
                result = normed * (1.0 + pick(1, columns)) + pick(0, columns)
                y[kind, j, g * padded : g * padded + frame, :] = result.astype(BF16)

    def project(kind, which, target):
        target[...] = jnp.zeros_like(target)

        @pl.loop(0, n_head)
        def _(j):
            begin = pl.multiple_of(j * shard, shard)
            target[...] += jnp.dot(
                y[kind, j], w_vmem[which, pl.ds(begin, shard), :], preferred_element_type=F32
            )

    lanes = lax.broadcasted_iota(jnp.int32, (rows, HD), 1)

    def to_link(stats):
        tall = jnp.concatenate([stats, jnp.zeros((link_rows - rows, HD), F32)], axis=0)
        return tall.T[:16, :]

    def from_link(flat):
        tall = jnp.concatenate([flat, jnp.zeros((HD - 16, link_rows), F32)], axis=0)
        return tall.T[:rows, :]

    def share_squares(kind, values):
        squares = jnp.sum(values * values, axis=-1, keepdims=True)
        flat = to_link(jnp.broadcast_to(squares, (rows, HD)))
        ss_send[kind] = flat
        copies = []
        for step in range(1, n_head):
            to = lax.rem(head + step, n_head)
            copies.append(
                remote(
                    ss_send.at[kind], ss_recv.at[kind, head], ss_send_sem.at[kind, step],
                    ss_recv_sem.at[kind, head], "head", to,
                )
            )
            copies[-1].start()
        return copies, flat

    def total_squares(kind, squares):
        for step in range(1, n_head):
            source = lax.rem(head + step, n_head)
            remote(
                ss_send.at[kind], ss_recv.at[kind, source], ss_send_sem.at[kind, step],
                ss_recv_sem.at[kind, source], "head", source,
            ).wait_recv()
            squares = squares + ss_recv[kind, source]
        return from_link(lax.rsqrt(squares / width + epsilon))[:, 0:1]

    in_copies[0].wait()
    in_copies[2].wait()
    forwards = gather_x(0)
    modulate(0, controls[0])
    w_copies[0].wait()
    project(0, 0, acc)
    ss_copies, squares = share_squares(0, acc[...])
    w_copies[1].wait()
    project(0, 1, acc_b)
    more, key_squares = share_squares(1, acc_b[...])
    ss_copies += more
    inverse = total_squares(0, squares)
    for g in range(groups):
        at = slice(g * padded, (g + 1) * padded)
        for h in range(heads):
            cols = slice(h * HD, (h + 1) * HD)
            normed = acc[at, cols] * inverse[at, :] * q_gain[cols][None, :]
            q_buf[seq, at, cols] = rotate(normed, caches + g, padded).astype(BF16)

    def q_copy(source, send, to):
        return remote(q_buf.at[source], q_buf.at[source], send, q_recv_sem.at[source], "seq", to)

    q_sends = []
    for step in range(1, n_z):
        q_sends.append(q_copy(seq, q_send_sem.at[step], partner(step) * NX + x))
        q_sends[-1].start()
    q_sends.append(q_copy(seq, q_fwd_sem.at[0], mate_x))
    q_sends[-1].start()

    w_copies[2].wait()
    project(0, 2, acc)
    inverse = total_squares(1, key_squares)
    for g in range(groups):
        at = slice(g * padded, (g + 1) * padded)
        place = slice((caches + g) * frame, (caches + g + 1) * frame)
        v32[place, :] = acc[at, :][:frame, :]
        for h in range(heads):
            cols = slice(h * HD, (h + 1) * HD)
            normed = acc_b[at, cols] * inverse[at, :] * k_gain[cols][None, :]
            k32[place, cols] = rotate(normed, caches + g, padded)[:frame, :]
    kb[...] = k32[...].astype(BF16)
    vb[...] = v32[...].astype(BF16)

    def pass_on(step):
        source = source_z(step) * NX + x
        q_copy(source, q_send_sem.at[0], mate_x).wait_recv()
        q_copy(source, q_fwd_sem.at[step], mate_x).start()

    in_copies[1].wait()
    forwards += gather_x(1)
    modulate(1, jnp.int32(0))
    if n_z > 1:
        pass_on(1)
    project(1, 1, acc_b)
    more, clean_squares = share_squares(2, acc_b[...])
    ss_copies += more

    sharp = HD ** (-0.5) * 1.4426950408889634
    last = key_rows - HD
    column = lax.broadcasted_iota(jnp.int32, (NX * rows, HD), 1) + last
    wide = lax.broadcasted_iota(jnp.int32, (NX * rows, HD), 1)

    def attend(there, slot):
        stats = jnp.zeros((NX * rows, HD), F32)
        queries = q_buf[pl.ds(there, NX)].reshape(NX * rows, inner)
        for h in range(heads):
            cols = slice(h * HD, (h + 1) * HD)
            scores = lax.dot_general(
                queries[:, cols], kb[:, cols], (((1,), (1,)), ((), ())),
                preferred_element_type=F32,
            )
            edge = jnp.where(column < n_keys, scores[:, last:], -3.0e38)
            scores = jnp.concatenate([scores[:, :last], edge], axis=1)
            top = jnp.max(scores, axis=-1, keepdims=True)
            weights = jnp.exp2((scores - top) * sharp)
            total = jnp.sum(weights, axis=-1, keepdims=True)
            sums = jnp.dot(weights.astype(BF16), vb[:, cols], preferred_element_type=F32)
            own_part[slot, :, :, cols] = sums.reshape(NX, rows, HD)
            stats = jnp.where(wide == h, top, stats)
            stats = jnp.where(wide == 8 + h, total, stats)
        own_stat[slot] = stats.reshape(NX, rows, HD)

    def mate_copy(step):
        return (
            remote(
                part_mate.at[step], mate_in.at[step], m_send_sem.at[step], m_recv_sem.at[step],
                "seq", mate_x,
            ),
            remote(
                stat_mate.at[step], mate_stat.at[step], mt_send_sem.at[step],
                mt_recv_sem.at[step], "seq", mate_x,
            ),
        )

    def part_copy(from_z, to_z):
        to = to_z * NX + x
        return (
            remote(
                part_send.at[to_z], part_recv.at[from_z], p_send_sem.at[to_z],
                p_recv_sem.at[from_z], "seq", to,
            ),
            remote(
                stat_send.at[to_z], stat_recv.at[from_z], t_send_sem.at[to_z],
                t_recv_sem.at[from_z], "seq", to,
            ),
        )

    def merge(done):
        slot = lax.rem(done, 2)
        to_z = source_z(done)
        for copy in mate_copy(done):
            copy.wait_recv()
        mine = own_stat[slot, x]
        other = from_link(mate_stat[done])
        top = jnp.maximum(mine, other)
        weight = jnp.exp2((mine - top) * sharp)
        weight_other = jnp.exp2((other - top) * sharp)
        total = weight * pltpu.roll(mine, HD - 8, 1) + weight_other * pltpu.roll(other, HD - 8, 1)
        for h in range(heads):
            cols = slice(h * HD, (h + 1) * HD)
            part_send[to_z, :, cols] = (
                own_part[slot, x, :, cols] * weight[:, h : h + 1]
                + mate_in[done, :, cols].astype(F32) * weight_other[:, h : h + 1]
            ).astype(BF16)
        stat_send[to_z] = to_link(jnp.where(lanes < 8, top, pltpu.roll(total, 8, 1)))

    @pl.loop(0, n_z)
    def _(step):
        there = source_z(step) * NX
        q_copy(there + (1 - x), q_send_sem.at[0], mate_x).wait_recv()
        slot = lax.rem(step, 2)
        attend(there, slot)
        part_mate[step] = own_part[slot, 1 - x].astype(BF16)
        stat_mate[step] = to_link(own_stat[slot, 1 - x])
        for copy in mate_copy(step):
            copy.start()

        @pl.when(step + 2 < n_z)
        def _():
            pass_on(step + 2)

        @pl.when(step > 0)
        def _():
            merge(step - 1)

            @pl.when(step > 1)
            def _():
                for copy in part_copy(z, source_z(step - 1)):
                    copy.start()

    project(1, 2, acc)
    inverse = total_squares(2, clean_squares)
    for g in range(groups):
        at = slice(g * padded, (g + 1) * padded)
        normed = acc_b[at, :] * inverse[at, :] * k_gain[...][None, :]
        fresh_keys[g] = normed[:frame, :].astype(BF16)
        fresh_values[g] = acc[at, :][:frame, :].astype(BF16)

    merge(n_z - 1)
    if n_z > 1:
        for copy in part_copy(z, source_z(n_z - 1)):
            copy.start()
    part_recv[z] = part_send[z]
    stat_recv[z] = stat_send[z]

    @pl.loop(1, n_z)
    def _(c):
        source = lax.rem(z + c, n_z)
        for copy in part_copy(source, source):
            copy.wait_recv()

    stats = [from_link(stat_recv[j]) for j in range(n_z)]
    top = stats[0]
    for stat in stats[1:]:
        top = jnp.maximum(top, stat)
    total = jnp.zeros((rows, HD), F32)
    acc[...] = jnp.zeros_like(acc)
    for j in range(n_z):
        weight = jnp.exp2((stats[j] - top) * sharp)
        total = total + weight * pltpu.roll(stats[j], HD - 8, 1)
        for h in range(heads):
            cols = slice(h * HD, (h + 1) * HD)
            acc[:, cols] += part_recv[j, :, cols].astype(F32) * weight[:, h : h + 1]
    for h in range(heads):
        cols = slice(h * HD, (h + 1) * HD)
        result = (acc[:, cols] / total[:, h : h + 1]).astype(BF16)
        for g in range(groups):
            out_ref[g, :, cols] = result[g * padded : g * padded + frame, :]

    for copy in x_sends + forwards + ss_copies + q_sends:
        copy.wait_send()

    @pl.loop(1, n_z)
    def _(step):
        q_copy(source_z(step) * NX + x, q_fwd_sem.at[step], mate_x).wait_send()

    @pl.loop(1, n_z)
    def _(c):
        to_z = lax.rem(z + c, n_z)
        for copy in part_copy(z, to_z):
            copy.wait_send()

    @pl.loop(0, n_z)
    def _(step):
        for copy in mate_copy(step):
            copy.wait_send()


def write_kernel(controls, keys, values, fresh_keys, fresh_values, new_keys, new_values):
    caches, groups = keys.shape[0], fresh_keys.shape[0]
    rolling = caches - controls[2]
    targets = [controls[2] + lax.rem(controls[1] + g, rolling) for g in range(groups)]
    for old, fresh, new in ((keys, fresh_keys, new_keys), (values, fresh_values, new_values)):
        for f in range(caches):
            kept = old[f]
            for g in range(groups):
                kept = jnp.where(targets[g] == f, fresh[g], kept)
            new[f] = kept


def body(n_seq, n_head, hidden, clean, w_query, w_key, w_value, q_gain, k_gain, keys, values,
         modulation, controls, frame_pos):
    groups, frame, shard = hidden.shape
    caches = keys.shape[0]
    inner = w_query.shape[1]
    padded = frame
    rows = groups * padded
    key_rows = -(-((caches + groups) * frame) // 128) * 128
    half = HD // 2
    time_pairs = (HD - 4 * (HD // 6)) // 2
    pair = np.arange(half)
    exponent = np.where(pair < time_pairs, pair / time_pairs, (pair - time_pairs) / (half - time_pairs))
    line = np.power(10000.0, -exponent).astype(np.float32)
    frequency = jnp.asarray(np.tile(np.concatenate([line, line])[None, :], (8, 1)))
    vmem = pl.BlockSpec(memory_space=pltpu.VMEM)
    smem = pl.BlockSpec(memory_space=pltpu.SMEM)
    hbm = pl.BlockSpec(memory_space=pl.ANY)
    dma = pltpu.SemaphoreType.DMA
    n_z = n_seq // NX
    link_rows = -(-rows // 128) * 128
    fresh = jax.ShapeDtypeStruct((groups, frame, inner), BF16)
    out, fresh_keys, fresh_values = pl.pallas_call(
        functools.partial(kernel, n_seq, n_head),
        out_shape=(fresh, fresh, fresh),
        in_specs=[hbm, hbm, hbm, hbm, hbm, vmem, vmem, hbm, hbm, hbm, vmem, smem, smem],
        out_specs=(vmem, vmem, vmem),
        scratch_shapes=[
            pltpu.VMEM((3,) + w_query.shape, BF16),
            pltpu.VMEM(modulation.shape, F32),
            pltpu.VMEM(keys.shape, BF16),
            pltpu.VMEM(values.shape, BF16),
            pltpu.VMEM((2, n_head, groups, frame, shard), BF16),
            pltpu.VMEM((2, n_head, rows, shard), BF16),
            pltpu.VMEM((rows, inner), F32),
            pltpu.VMEM((rows, inner), F32),
            pltpu.VMEM((caches + groups, 2, padded, HD), F32),
            pltpu.VMEM((key_rows, inner), F32),
            pltpu.VMEM((key_rows, inner), F32),
            pltpu.VMEM((key_rows, inner), BF16),
            pltpu.VMEM((key_rows, inner), BF16),
            pltpu.VMEM((n_seq, rows, inner), BF16),
            pltpu.VMEM((n_z, rows, inner), BF16),
            pltpu.VMEM((n_z, rows, inner), BF16),
            pltpu.VMEM((n_z, 16, link_rows), F32),
            pltpu.VMEM((n_z, 16, link_rows), F32),
            pltpu.VMEM((3, 16, link_rows), F32),
            pltpu.VMEM((3, n_head, 16, link_rows), F32),
            pltpu.VMEM((2, NX, rows, inner), F32),
            pltpu.VMEM((2, NX, rows, HD), F32),
            pltpu.VMEM((n_z, rows, inner), BF16),
            pltpu.VMEM((n_z, 16, link_rows), F32),
            pltpu.VMEM((n_z, rows, inner), BF16),
            pltpu.VMEM((n_z, 16, link_rows), F32),
            dma((3,)),
            dma((5,)),
            dma((2, n_head)),
            dma((2, n_head)),
            dma((2, n_head)),
            dma((3, n_head)),
            dma((3, n_head)),
            dma((n_seq,)),
            dma((n_seq,)),
            dma((n_seq,)),
            dma((n_z,)),
            dma((n_z,)),
            dma((n_z,)),
            dma((n_z,)),
            dma((n_z,)),
            dma((n_z,)),
            dma((n_z,)),
            dma((n_z,)),
        ],
        compiler_params=pltpu.CompilerParams(
            collective_id=0, has_side_effects=True, vmem_limit_bytes=60 * 1024 * 1024
        ),
        name="block",
    )(hidden, clean, w_query, w_key, w_value, q_gain, k_gain, keys, values,
      modulation, frequency, controls, frame_pos)
    new_keys, new_values = pl.pallas_call(
        write_kernel,
        out_shape=(
            jax.ShapeDtypeStruct(keys.shape, BF16),
            jax.ShapeDtypeStruct(values.shape, BF16),
        ),
        in_specs=[smem, vmem, vmem, vmem, vmem],
        out_specs=(vmem, vmem),
        name="write",
    )(controls, keys, values, fresh_keys, fresh_values)
    return out, new_keys, new_values


def solution(mesh):
    split = P(None, "seq", "head")
    columns = P(None, "head")
    in_specs = (
        split, split, columns, columns, columns, P("head"), P("head"), split, split, P(), P(), P(),
    )
    step = functools.partial(body, mesh.shape["seq"], mesh.shape["head"])
    return jax.shard_map(
        step, mesh=mesh, in_specs=in_specs, out_specs=(split, split, split), check_vma=False
    )
```
